256 devices in a mesh: dp: 32 (over z_hi, x, core), seq: 8 (over y, z_lo).
Axes of the slice: x: 4, y: 4, z: 8 (z_hi: 4, z_lo: 2; z = z_hi * 2 + z_lo), core: 2. Of those that a mesh axis runs over, the one named last changes fastest.
Arguments:
- q_proj: bfloat16 [32, 1024, 4096], P('dp', 'seq'), may hold values from -200 to 200
- k_proj: bfloat16 [32, 1024, 512], P('dp', 'seq'), may hold values from -6 to 6
- v_proj: bfloat16 [32, 1024, 512], P('dp', 'seq'), may hold values from -6 to 6
- cache_k: bfloat16 [32, 1024, 512], P('dp', 'seq'), may hold values from -6 to 6
- cache_v: bfloat16 [32, 1024, 512], P('dp', 'seq'), may hold values from -6 to 6
- bias_q: bfloat16 [4096], replicated, may hold values from -3 to 3
- bias_k: bfloat16 [512], replicated, may hold values from -3 to 3
- bias_v: bfloat16 [512], replicated, may hold values from -3 to 3
- start: int32 [32], P('dp'), may hold values from 256 to 1024, as said below
- dout: bfloat16 [32, 1024, 4096], P('dp', 'seq'), may hold values from -6 to 6
Outputs:
- attn_out: bfloat16 [32, 1024, 4096], P('dp', 'seq')
- grad_q: bfloat16 [32, 1024, 4096], P('dp', 'seq')
- grad_k: bfloat16 [32, 1024, 512], P('dp', 'seq')
- grad_v: bfloat16 [32, 1024, 512], P('dp', 'seq')
- grad_bias_q: float32 [4096], replicated
- grad_bias_k: float32 [512], replicated
- grad_bias_v: float32 [512], replicated
The draws below stay inside these ranges and needn't reach their ends.
Inputs may be any that keep to these rules, and one draw needn't show every extreme that they name: Cache slots at and beyond start hold no prefix; some sequence has a full prefix of 1024 slots.
All inputs are finite; a program needn't handle non-finite values.
Results may differ from the reference program's by a relative error of at most 0.04.
The reference program's roundings to bfloat16 on the way count: a program that leaves them out, or rounds other values in their place, can miss the bound.
Values may be sent and summed in bfloat16 or wider, within the bound.
A program may use at most 128 MiB of HBM per device.

```python
import jax
import jax.numpy as jnp
from jax import lax

HQ = 32
KV = 4
HD = 128
PREFIX = 1024
GROUP = 8
LEN = 1024
SEQS = 32


def draw_q_proj(key, part):
    first_key = jax.random.fold_in(jax.random.fold_in(key, 11), 0)
    values = jax.random.normal(first_key, (SEQS, LEN, HQ * HD), jnp.float32)
    values = jnp.clip(values, -6.0, 6.0)
    return values.astype(jnp.bfloat16)


def draw_start(key, part):
    values = jax.random.randint(jax.random.fold_in(key, 23), (SEQS,), PREFIX // 4, PREFIX + 1, dtype=jnp.int32)
    return values.at[0].set(PREFIX)


def steps_of(stream_key, shape, cuts, least, largest):
    loudness = 1.0
    for dim, blocks in cuts:
        draws = jax.random.uniform(jax.random.fold_in(jax.random.fold_in(stream_key, 6), dim), (blocks,), jnp.float32, least / len(cuts), largest / len(cuts))
        loudness = loudness * jnp.repeat(jnp.exp(draws), shape[dim] // blocks).reshape((-1,) + (1,) * (len(shape) - 1 - dim))
    return loudness


def bell_draw(rng, shape, deviation, limit, cuts=(), kind=jnp.bfloat16):
    entries = deviation * jax.random.normal(rng, shape, jnp.float32)
    if cuts:
        entries = entries * steps_of(rng, shape, cuts, -0.22, 0.18)
    return jnp.clip(entries, -limit, limit).astype(kind)


def setup_inputs(seed: int = 0) -> dict:
    splits = jax.random.split(jax.random.key(seed), 11)
    q_proj = draw_q_proj(jax.random.fold_in(splits[10], 71), 0)
    k_proj = bell_draw(splits[1], (SEQS, LEN, KV * HD), 1.0, 6.0, ((0, 32), (1, 8)))
    v_proj = bell_draw(splits[2], (SEQS, LEN, KV * HD), 1.0, 6.0, ((0, 32), (1, 8)))
    cache_k = bell_draw(splits[3], (SEQS, PREFIX, KV * HD), 1.0, 6.0, ((0, 32), (1, 8)))
    cache_v = bell_draw(splits[4], (SEQS, PREFIX, KV * HD), 1.0, 6.0, ((0, 32), (1, 8)))
    bias_q = bell_draw(splits[5], (HQ * HD,), 0.5, 3.0)
    bias_k = bell_draw(splits[6], (KV * HD,), 0.5, 3.0)
    bias_v = bell_draw(splits[7], (KV * HD,), 0.5, 3.0)
    start = draw_start(jax.random.fold_in(splits[10], 71), 0)
    dout = bell_draw(splits[9], (SEQS, LEN, HQ * HD), 1.0, 6.0, ((0, 32), (1, 8)))
    return dict(q_proj=q_proj, k_proj=k_proj, v_proj=v_proj, cache_k=cache_k, cache_v=cache_v, bias_q=bias_q, bias_k=bias_k, bias_v=bias_v, start=start, dout=dout)


def rotary_tables(positions, width):
    half = width // 2
    freqs = jnp.exp(-(2.0 * jnp.arange(half, dtype=jnp.float32) / width) * jnp.log(jnp.float32(1.0e6)))
    angles = positions.astype(jnp.float32)[:, None] * freqs[None, :]
    cosine = jnp.concatenate([jnp.cos(angles), jnp.cos(angles)], axis=1)
    sine = jnp.concatenate([jnp.sin(angles), jnp.sin(angles)], axis=1)
    return cosine[:, None, :], sine[:, None, :]


def rotary(values, positions):
    cosine, sine = rotary_tables(positions, values.shape[2])
    half = values.shape[2] // 2
    turned = jnp.concatenate([-values[:, :, half:], values[:, :, :half]], axis=2)
    return values * cosine + turned * sine


def rotary_back(grads, positions):
    cosine, sine = rotary_tables(positions, grads.shape[2])
    half = grads.shape[2] // 2
    scaled = grads * sine
    turned = jnp.concatenate([scaled[:, :, half:], -scaled[:, :, :half]], axis=2)
    return grads * cosine + turned


def attend(queries, cotangent, keys, values, first, row_zero, prefix):
    rows, heads, width = queries.shape
    key_count = keys.shape[0]
    slab = key_count - prefix
    head_block = max(1, min(512 // rows, GROUP, heads))
    row_block = min(rows, 512)
    scale = width ** -0.5
    key_index = jnp.arange(key_count, dtype=jnp.int32)

    def head_step(carry, head_slot):
        key_acc, value_acc = carry
        head_zero = head_slot * head_block
        owner = head_zero // GROUP
        key_one = lax.dynamic_index_in_dim(keys, owner, 1, keepdims=False).astype(jnp.float32)
        value_one = lax.dynamic_index_in_dim(values, owner, 1, keepdims=False).astype(jnp.float32)
        query_part = lax.dynamic_slice_in_dim(queries, head_zero, head_block, 1)
        cot_part = lax.dynamic_slice_in_dim(cotangent, head_zero, head_block, 1)

        def row_step(inner, row_slot):
            grad_key, grad_value = inner
            offset = row_slot * row_block
            query_rows = lax.dynamic_slice_in_dim(query_part, offset, row_block, 0).astype(jnp.float32)
            cot_rows = lax.dynamic_slice_in_dim(cot_part, offset, row_block, 0).astype(jnp.float32)
            query_index = row_zero + offset + jnp.arange(row_block, dtype=jnp.int32)
            allowed = jnp.where(key_index[None, :] < prefix, key_index[None, :] < first,
                                (key_index[None, :] - prefix) <= query_index[:, None])
            scores = jnp.einsum('rhd,kd->hrk', query_rows, key_one) * scale
            scores = jnp.where(allowed[None], scores, -1.0e30)
            highest = jnp.max(scores, axis=-1, keepdims=True)
            expo = jnp.exp(scores - highest)
            probs = expo / jnp.sum(expo, axis=-1, keepdims=True)
            probs_b = probs.astype(jnp.bfloat16)
            output = jnp.einsum('hrk,kd->rhd', probs_b.astype(jnp.float32), value_one).astype(jnp.bfloat16)
            delta = jnp.sum(cot_rows * output.astype(jnp.float32), axis=-1).T
            dprobs = jnp.einsum('rhd,kd->hrk', cot_rows, value_one)
            dscore = (probs * (dprobs - delta[:, :, None])).astype(jnp.bfloat16)
            dscore_f = dscore.astype(jnp.float32)
            grad_query = (jnp.einsum('hrk,kd->rhd', dscore_f, key_one) * scale).astype(jnp.bfloat16)
            grad_key = grad_key + jnp.einsum('hrk,rhd->kd', dscore_f[:, :, prefix:], query_rows) * scale
            grad_value = grad_value + jnp.einsum('hrk,rhd->kd', probs_b[:, :, prefix:].astype(jnp.float32), cot_rows)
            return (grad_key, grad_value), (output, grad_query)

        empty = jnp.zeros((slab, width), jnp.float32)
        (grad_key, grad_value), (outputs, grads) = lax.scan(row_step, (empty, empty),
                                                            jnp.arange(rows // row_block, dtype=jnp.int32))
        outputs = outputs.reshape(rows, head_block, width)
        grads = grads.reshape(rows, head_block, width)
        old_key = lax.dynamic_index_in_dim(key_acc, owner, 1, keepdims=False)
        old_value = lax.dynamic_index_in_dim(value_acc, owner, 1, keepdims=False)
        key_acc = lax.dynamic_update_index_in_dim(key_acc, old_key + grad_key, owner, 1)
        value_acc = lax.dynamic_update_index_in_dim(value_acc, old_value + grad_value, owner, 1)
        return (key_acc, value_acc), (outputs, grads)

    zeros_kv = jnp.zeros((slab, keys.shape[1], width), jnp.float32)
    (key_acc, value_acc), (outputs, grads) = lax.scan(head_step, (zeros_kv, zeros_kv),
                                                      jnp.arange(heads // head_block, dtype=jnp.int32))
    outputs = jnp.transpose(outputs, (1, 0, 2, 3)).reshape(rows, heads, width)
    grads = jnp.transpose(grads, (1, 0, 2, 3)).reshape(rows, heads, width)
    return outputs, grads, key_acc, value_acc


def reference(q_proj, k_proj, v_proj, cache_k, cache_v, bias_q, bias_k, bias_v, start, dout):
    def one_sequence(items):
        query_in, key_in, value_in, cached_k, cached_v, first, cot = items
        positions = first + jnp.arange(LEN, dtype=jnp.int32)
        queries = rotary((query_in.astype(jnp.float32) + bias_q.astype(jnp.float32)).reshape(LEN, HQ, HD), positions).astype(jnp.bfloat16)
        keys = rotary((key_in.astype(jnp.float32) + bias_k.astype(jnp.float32)).reshape(LEN, KV, HD), positions).astype(jnp.bfloat16)
        values = (value_in.astype(jnp.float32) + bias_v.astype(jnp.float32)).astype(jnp.bfloat16).reshape(LEN, KV, HD)
        all_keys = jnp.concatenate([cached_k.reshape(PREFIX, KV, HD), keys], axis=0)
        all_values = jnp.concatenate([cached_v.reshape(PREFIX, KV, HD), values], axis=0)
        outputs, dq_rot, dk_rot, dv_all = attend(queries, cot.reshape(LEN, HQ, HD), all_keys, all_values, first, 0, PREFIX)
        grad_query = rotary_back(dq_rot.astype(jnp.float32), positions)
        grad_key = rotary_back(dk_rot, positions)
        return (outputs.reshape(LEN, HQ * HD), grad_query.astype(jnp.bfloat16).reshape(LEN, HQ * HD),
                grad_key.astype(jnp.bfloat16).reshape(LEN, KV * HD), dv_all.astype(jnp.bfloat16).reshape(LEN, KV * HD),
                jnp.sum(grad_query, axis=0).reshape(HQ * HD), jnp.sum(grad_key, axis=0).reshape(KV * HD),
                jnp.sum(dv_all, axis=0).reshape(KV * HD))

    results = lax.map(one_sequence, (q_proj, k_proj, v_proj, cache_k, cache_v, start, dout))
    return (results[0], results[1], results[2], results[3],
            jnp.sum(results[4], axis=0), jnp.sum(results[5], axis=0), jnp.sum(results[6], axis=0))
```

```python
import functools

import jax
import jax.numpy as jnp
import numpy as np
from jax import lax
from jax.experimental import pallas as pl
from jax.experimental.pallas import tpu as pltpu
from jax.sharding import PartitionSpec as P

HQ = 32
KV = 4
HD = 128
GROUP = 8
SCALE = float(HD**-0.5)
EXP2_SCALE = float(np.log2(np.e) * HD**-0.5)
f32 = jnp.float32
bf16 = jnp.bfloat16


def rotary_tables(positions):
    half = HD // 2
    freqs = jnp.exp(
        -(2.0 * jnp.arange(half, dtype=f32) / HD) * jnp.log(jnp.float32(1000000.0))
    )
    angles = positions.astype(f32)[:, None] * freqs[None, :]
    cosine, sine = jnp.cos(angles), jnp.sin(angles)
    return (
        jnp.concatenate([cosine, cosine], axis=1),
        jnp.concatenate([-sine, sine], axis=1),
    )


def dot(a, b, contract_a, contract_b):
    return lax.dot_general(
        a, b, (((contract_a,), (contract_b,)), ((), ())), preferred_element_type=f32
    )


def turn(x):
    return pltpu.roll(x, HD // 2, axis=1)


def attend_kernel(
    n,
    start_ref, q_ref, k_ref, v_ref, ck_ref, cv_ref, bq_ref, bk_ref, bv_ref, cos_ref, sin_ref, do_ref,
    out_ref, gq_ref, gk_ref, gv_ref, sums_ref,
    kv, rsend, rrecv, q_s, do_s, s_ref, p_ref, mask_ref, stat, norm, acc, q_t, do_t, do_n,
    kv_send, kv_recv, r_send, r_recv,
):
    me = lax.axis_index("seq")
    tokens = q_ref.shape[0]
    keys = n * tokens
    rows = GROUP * tokens

    barrier = pltpu.get_barrier_semaphore()

    def greet(i, _):
        pl.semaphore_signal(barrier, inc=1, device_id={"seq": lax.rem(me + i, n)}, device_id_type=pl.DeviceIdType.MESH)
        return 0

    lax.fori_loop(1, n, greet, 0)

    cosine, sine = cos_ref[...], sin_ref[...]
    for h in range(KV):
        cols = slice(h * HD, (h + 1) * HD)
        x = k_ref[:, cols].astype(f32) + bk_ref[:, cols].astype(f32)
        kv[h, 0, 1, me] = (x * cosine + turn(x) * sine).astype(bf16)
        kv[h, 1, 1, me] = (v_ref[:, cols].astype(f32) + bv_ref[:, cols].astype(f32)).astype(bf16)
        kv[h, 0, 0, me] = ck_ref[:, cols]
        kv[h, 1, 0, me] = cv_ref[:, cols]

    pl.semaphore_wait(barrier, n - 1)

    def kv_copy(h, owner, peer):
        block = kv.at[h, :, :, owner]
        return pltpu.make_async_remote_copy(
            src_ref=block, dst_ref=block, send_sem=kv_send.at[h, peer], recv_sem=kv_recv.at[h, owner],
            device_id={"seq": peer}, device_id_type=pl.DeviceIdType.MESH,
        )

    def r_copy(h, source, peer):
        return pltpu.make_async_remote_copy(
            src_ref=rsend.at[h, :, peer], dst_ref=rrecv.at[h, :, source],
            send_sem=r_send.at[h, peer], recv_sem=r_recv.at[h, source],
            device_id={"seq": peer}, device_id_type=pl.DeviceIdType.MESH,
        )

    def send_head(h, _):
        def send(i, _):
            kv_copy(h, me, lax.rem(me + i, n)).start()
            return 0

        return lax.fori_loop(1, n, send, 0)

    lax.fori_loop(0, KV, send_head, 0)

    row = lax.broadcasted_iota(jnp.int32, (tokens, keys), 0)
    col = lax.broadcasted_iota(jnp.int32, (tokens, keys), 1)
    mask_ref[0] = jnp.where(col < start_ref[0], 0.0, -1e30)
    mask_ref[1] = jnp.where(col <= row + me * tokens, 0.0, -1e30)

    def load_queries(h, _):
        for g in range(GROUP):
            cols = pl.ds(pl.multiple_of((h * GROUP + g) * HD, HD), HD)
            x = q_ref[:, cols].astype(f32) + bq_ref[:, cols].astype(f32)
            q_s[h, g * tokens : (g + 1) * tokens, :] = (x * cosine + turn(x) * sine).astype(bf16)
            do_s[h, g * tokens : (g + 1) * tokens, :] = do_ref[:, cols]
        return 0

    lax.fori_loop(0, KV, load_queries, 0)

    def head(h, _):
        def await_keys(i, _):
            source = lax.rem(me + i, n)
            kv_copy(h, source, source).wait_recv()
            return 0

        lax.fori_loop(1, n, await_keys, 0)

        q_t[...] = q_s[h].T
        stat[...] = jnp.full(stat.shape, -3e38, f32)

        def score(part, _):
            s = dot(q_s[h], kv[h, 0, part].reshape(keys, HD), 1, 1)
            s = (s.reshape(GROUP, tokens, keys) + mask_ref[part][None]).reshape(rows, keys)
            s_ref[part] = s
            m = stat[...]
            for t in range(keys // HD):
                m = jnp.maximum(m, s[:, t * HD : (t + 1) * HD])
            stat[...] = m
            return 0

        lax.fori_loop(0, 2, score, 0)
        stat[...] = jnp.broadcast_to(jnp.max(stat[...], axis=1, keepdims=True), stat.shape)
        norm[...] = jnp.zeros(norm.shape, f32)
        acc[...] = jnp.zeros(acc.shape, f32)

        def weigh(part, _):
            m = stat[...]
            pieces = [
                jnp.exp2((s_ref[part, :, t * HD : (t + 1) * HD] - m) * EXP2_SCALE)
                for t in range(keys // HD)
            ]
            norm[...] += functools.reduce(lambda a, b: a + b, pieces)
            p = jnp.concatenate([x.astype(bf16) for x in pieces], axis=1)
            p_ref[part] = p
            acc[...] += dot(p, kv[h, 1, part].reshape(keys, HD), 1, 0)
            return 0

        lax.fori_loop(0, 2, weigh, 0)
        inverse = 1.0 / jnp.sum(norm[...], axis=1, keepdims=True)
        out = (acc[...] * inverse).astype(bf16)
        for g in range(GROUP):
            cols = pl.ds(pl.multiple_of((h * GROUP + g) * HD, HD), HD)
            out_ref[:, cols] = out[g * tokens : (g + 1) * tokens]
        scaled = (do_s[h].astype(f32) * inverse).astype(bf16)
        do_n[...] = scaled
        do_t[...] = scaled.T
        delta = jnp.sum(scaled.astype(f32) * out.astype(f32), axis=1, keepdims=True)
        stat[...] = jnp.broadcast_to(delta, stat.shape)
        acc[...] = jnp.zeros(acc.shape, f32)

        def score_grad(part):
            dp = dot(do_n[...], kv[h, 1, part].reshape(keys, HD), 1, 1)
            delta = stat[...]
            ds = jnp.concatenate(
                [
                    (
                        (dp[:, t * HD : (t + 1) * HD] - delta)
                        * p_ref[part, :, t * HD : (t + 1) * HD].astype(f32)
                    ).astype(bf16)
                    for t in range(keys // HD)
                ],
                axis=1,
            )
            acc[...] += dot(ds, kv[h, 0, part].reshape(keys, HD), 1, 0)
            return ds

        ds = score_grad(1)
        rsend[h, 0] = (dot(q_t[...], ds, 1, 0).T * SCALE).astype(bf16).reshape(n, tokens, HD)
        rsend[h, 1] = dot(do_t[...], p_ref[1], 1, 0).T.astype(bf16).reshape(n, tokens, HD)

        def send_back(peer, _):
            r_copy(h, me, peer).start()
            return 0

        lax.fori_loop(0, me, send_back, 0)
        score_grad(0)
        dq = (acc[...] * SCALE).astype(bf16).astype(f32)
        for g in range(GROUP):
            cols = pl.ds(pl.multiple_of((h * GROUP + g) * HD, HD), HD)
            x = dq[g * tokens : (g + 1) * tokens]
            gq = x * cosine - turn(x) * sine
            gq_ref[:, cols] = gq.astype(bf16)
            sums_ref[h, g : g + 1, :] = jnp.sum(gq, axis=0, keepdims=True)
        return 0

    lax.fori_loop(0, KV, head, 0)

    sums_ref[KV] = jnp.zeros((GROUP, HD), f32)
    for h in range(KV):
        cols = slice(h * HD, (h + 1) * HD)

        def gather(source, total):
            r_copy(h, source, source).wait_recv()
            return total + rrecv[h, :, source].astype(f32)

        total = lax.fori_loop(me + 1, n, gather, rsend[h, :, me].astype(f32))
        gk = total[0] * cosine - turn(total[0]) * sine
        gk_ref[:, cols] = gk.astype(bf16)
        gv_ref[:, cols] = total[1].astype(bf16)
        sums_ref[KV, h : h + 1, :] = jnp.sum(gk, axis=0, keepdims=True)
        sums_ref[KV, KV + h : KV + h + 1, :] = jnp.sum(total[1], axis=0, keepdims=True)

    def drain_head(h, _):
        def drain_kv(i, _):
            kv_copy(h, me, lax.rem(me + i, n)).wait_send()
            return 0

        def drain_r(peer, _):
            r_copy(h, me, peer).wait_send()
            return 0

        lax.fori_loop(1, n, drain_kv, 0)
        return lax.fori_loop(0, me, drain_r, 0)

    lax.fori_loop(0, KV, drain_head, 0)


def sum_kernel(n, m, x_ref, out_ref, first, second, s1, r1, s2, r2, s3, r3):
    me, mine = lax.axis_index("seq"), lax.axis_index("dp")
    barrier = pltpu.get_barrier_semaphore()

    def greet(axis, size, index):
        def one(i, _):
            pl.semaphore_signal(barrier, inc=1, device_id={axis: lax.rem(index + i, size)}, device_id_type=pl.DeviceIdType.MESH)
            return 0

        lax.fori_loop(1, size, one, 0)

    greet("seq", n, me)
    greet("dp", m, mine)
    pl.semaphore_wait(barrier, n + m - 2)

    def exchange(axis, size, index, source, target, send, recv):
        def copy(owner, peer):
            return pltpu.make_async_remote_copy(
                src_ref=source(peer), dst_ref=target(owner), send_sem=send.at[peer], recv_sem=recv.at[owner],
                device_id={axis: peer}, device_id_type=pl.DeviceIdType.MESH,
            )

        def begin(i, _):
            copy(index, lax.rem(index + i, size)).start()
            return 0

        def arrive(i, _):
            peer = lax.rem(index + i, size)
            copy(peer, peer).wait_recv()
            return 0

        def leave(i, _):
            copy(index, lax.rem(index + i, size)).wait_send()
            return 0

        lax.fori_loop(1, size, begin, 0)
        lax.fori_loop(1, size, arrive, 0)
        return lambda: lax.fori_loop(1, size, leave, 0)

    first[me] = x_ref[me]
    leave_first = exchange("seq", n, me, lambda peer: x_ref.at[peer], lambda owner: first.at[owner], s1, r1)
    second[mine] = jnp.sum(first[...], axis=0)
    leave_second = exchange("dp", m, mine, lambda peer: second.at[mine], lambda owner: second.at[owner], s2, r2)
    out_ref[me] = jnp.sum(second[...], axis=0)
    leave_third = exchange("seq", n, me, lambda peer: out_ref.at[me], lambda owner: out_ref.at[owner], s3, r3)
    leave_first()
    leave_second()
    leave_third()


def body(n, m, q_proj, k_proj, v_proj, cache_k, cache_v, bias_q, bias_k, bias_v, start, dout):
    rank = lax.axis_index("seq")
    tokens = q_proj.shape[1]
    keys, rows = n * tokens, GROUP * tokens
    cosine, sine = rotary_tables(start[0] + rank * tokens + jnp.arange(tokens, dtype=jnp.int32))
    vmem = pl.BlockSpec(memory_space=pltpu.VMEM)
    dma = pltpu.SemaphoreType.DMA
    out, grad_q, grad_k, grad_v, sums = pl.pallas_call(
        functools.partial(attend_kernel, n),
        out_shape=[
            jax.ShapeDtypeStruct((tokens, HQ * HD), bf16),
            jax.ShapeDtypeStruct((tokens, HQ * HD), bf16),
            jax.ShapeDtypeStruct((tokens, KV * HD), bf16),
            jax.ShapeDtypeStruct((tokens, KV * HD), bf16),
            jax.ShapeDtypeStruct((KV + 1, GROUP, HD), f32),
        ],
        in_specs=[pl.BlockSpec(memory_space=pltpu.SMEM)] + [vmem] * 11,
        out_specs=[vmem] * 5,
        scratch_shapes=[
            pltpu.VMEM((KV, 2, 2, n, tokens, HD), bf16),
            pltpu.VMEM((KV, 2, n, tokens, HD), bf16),
            pltpu.VMEM((KV, 2, n, tokens, HD), bf16),
            pltpu.VMEM((KV, rows, HD), bf16),
            pltpu.VMEM((KV, rows, HD), bf16),
            pltpu.VMEM((2, rows, keys), f32),
            pltpu.VMEM((2, rows, keys), bf16),
            pltpu.VMEM((2, tokens, keys), f32),
            pltpu.VMEM((rows, HD), f32),
            pltpu.VMEM((rows, HD), f32),
            pltpu.VMEM((rows, HD), f32),
            pltpu.VMEM((HD, rows), bf16),
            pltpu.VMEM((HD, rows), bf16),
            pltpu.VMEM((rows, HD), bf16),
            dma((KV, n)),
            dma((KV, n)),
            dma((KV, n)),
            dma((KV, n)),
        ],
        compiler_params=pltpu.CompilerParams(collective_id=0, has_side_effects=True, vmem_limit_bytes=60 << 20),
        name="attend",
    )(
        start, q_proj[0], k_proj[0], v_proj[0], cache_k[0], cache_v[0],
        bias_q[None], bias_k[None], bias_v[None], cosine, sine, dout[0],
    )
    slots = (KV + 1) * GROUP // n
    packed = jnp.pad(sums.reshape(n, slots, HD), ((0, 0), (0, 8 - slots), (0, 0)))
    total = pl.pallas_call(
        functools.partial(sum_kernel, n, m),
        out_shape=jax.ShapeDtypeStruct((n, 8, HD), f32),
        in_specs=[vmem],
        out_specs=vmem,
        scratch_shapes=[pltpu.VMEM((n, 8, HD), f32), pltpu.VMEM((m, 8, HD), f32)]
        + [dma((n,)), dma((n,)), dma((m,)), dma((m,)), dma((n,)), dma((n,))],
        compiler_params=pltpu.CompilerParams(collective_id=1, has_side_effects=True),
        name="bias_sums",
    )(packed)
    total = total[:, :slots].reshape((KV + 1) * GROUP * HD)
    split = HQ * HD
    return (
        out[None], grad_q[None], grad_k[None], grad_v[None],
        total[:split], total[split : split + KV * HD], total[split + KV * HD :],
    )


def solution(mesh):
    n, m = mesh.shape["seq"], mesh.shape["dp"]
    tokens = P("dp", "seq", None)
    return jax.shard_map(
        functools.partial(body, n, m),
        mesh=mesh,
        in_specs=(tokens, tokens, tokens, tokens, tokens, P(), P(), P(), P("dp"), tokens),
        out_specs=(tokens, tokens, tokens, tokens, P(), P(), P()),
        check_vma=False,
    )
```

```python
import functools

import jax
import jax.numpy as jnp
import numpy as np
from jax import lax
from jax.experimental import pallas as pl
from jax.experimental.pallas import tpu as pltpu
from jax.sharding import PartitionSpec as P

HQ = 32
KV = 4
HD = 128
GROUP = 8
SUMS = HQ + 2 * KV
SCALE = float(HD**-0.5)
EXP2_SCALE = float(np.log2(np.e) * HD**-0.5)
MESH = pl.DeviceIdType.MESH
f32 = jnp.float32
bf16 = jnp.bfloat16


def dot(a, b, contract_a, contract_b):
    return lax.dot_general(
        a, b, (((contract_a,), (contract_b,)), ((), ())), preferred_element_type=f32
    )


def turn(x):
    return pltpu.roll(x, HD // 2, axis=1)


def attend_kernel(
    n, inner, outer,
    start_ref, bias_ref, freq_ref, q_ref, k_ref, v_ref, ck_ref, cv_ref, do_ref,
    out_ref, gq_ref, gk_ref, gv_ref, sums_ref,
    kv, rsend, rrecv, q_s, do_s, s_ref, p_ref, mask_ref, stat, norm, acc, q_t, do_t, do_n, cos_s, sin_s,
    sum_a, sum_b, sum_c,
    kv_send, kv_recv, r_send, r_recv, a_send, a_recv, b_send, b_recv, c_send, c_recv,
):
    me, mine = lax.axis_index("seq"), lax.axis_index("dp")
    tokens = q_ref.shape[0]
    keys = n * tokens
    rows = GROUP * tokens
    ring = n // 2
    y, z = me // 2, lax.rem(me, 2)

    def place(dy, dz):
        return lax.rem(y + dy, ring) * 2 + lax.rem(z + dz, 2)

    up, down, far = place(1, 0), place(ring - 1, 0), place(2, 0)
    side, side_up, side_down, side_far = place(0, 1), place(1, 1), place(ring - 1, 1), place(2, 1)
    block, lane = mine // inner, lax.rem(mine, inner)

    barrier = pltpu.get_barrier_semaphore()

    def greet(device):
        pl.semaphore_signal(barrier, inc=1, device_id=device, device_id_type=MESH)

    def greet_seq(i, _):
        greet({"seq": lax.rem(me + i, n)})
        return 0

    def greet_inner(i, _):
        greet({"dp": block * inner + lax.rem(lane + i, inner)})
        return 0

    def greet_outer(i, _):
        greet({"dp": lax.rem(block + i, outer) * inner + lane})
        return 0

    lax.fori_loop(1, n, greet_seq, 0)
    lax.fori_loop(1, inner, greet_inner, 0)
    lax.fori_loop(1, outer, greet_outer, 0)

    flip = jnp.where(lax.broadcasted_iota(jnp.int32, (1, HD), 1) < HD // 2, -1.0, 1.0)

    def table(owner):
        at = pl.ds(pl.multiple_of(owner * tokens, tokens), tokens)
        position = start_ref[0] + owner * tokens + lax.broadcasted_iota(jnp.int32, (tokens, HD), 0)
        angle = position.astype(f32) * freq_ref[...]
        cos_s[at, :] = jnp.cos(angle)
        sin_s[at, :] = jnp.sin(angle) * flip

    table(me)
    own_rows = pl.ds(pl.multiple_of(me * tokens, tokens), tokens)
    cosine, sine = cos_s[own_rows, :], sin_s[own_rows, :]
    for h in range(KV):
        cols = slice(h * HD, (h + 1) * HD)
        x = k_ref[:, cols].astype(f32) + bias_ref[HQ + h : HQ + h + 1, :]
        kv[h, 0, 1, me] = (x * cosine + turn(x) * sine).astype(bf16)
        kv[h, 1, 1, me] = (v_ref[:, cols].astype(f32) + bias_ref[HQ + KV + h : HQ + KV + h + 1, :]).astype(bf16)
        kv[h, 0, 0, me] = ck_ref[:, cols]
        kv[h, 1, 0, me] = cv_ref[:, cols]

    pl.semaphore_wait(barrier, n + inner + outer - 3)

    def kv_copy(h, half, owner, peer, slot):
        part = kv.at[h, half, :, owner]
        return pltpu.make_async_remote_copy(
            src_ref=part, dst_ref=part, send_sem=kv_send.at[h, half, slot], recv_sem=kv_recv.at[h, half, owner],
            device_id={"seq": peer}, device_id_type=MESH,
        )

    def arrived(h, half, owner):
        kv_copy(h, half, owner, owner, 0).wait_recv()

    def r_copy(h, source, peer):
        return pltpu.make_async_remote_copy(
            src_ref=rsend.at[h, :, peer], dst_ref=rrecv.at[h, :, source],
            send_sem=r_send.at[h, peer], recv_sem=r_recv.at[h, source],
            device_id={"seq": peer}, device_id_type=MESH,
        )

    def send_own(h):
        for half in range(2):
            kv_copy(h, half, me, side, 0).start()
            kv_copy(h, half, me, up, 1).start()
            kv_copy(h, half, me, down, 2).start()

    def relay_near(h):
        for half in range(2):
            arrived(h, half, side)
            kv_copy(h, half, side, up, 3).start()
            kv_copy(h, half, side, down, 4).start()
            if half == 0:
                arrived(h, 0, down)
                kv_copy(h, 0, down, up, 5).start()
            else:
                arrived(h, 1, up)
                kv_copy(h, 1, up, down, 5).start()

    def relay_far(h):
        for half in range(2):
            arrived(h, half, far)
            kv_copy(h, half, far, side, 6).start()

    def await_half(h, half):
        arrived(h, half, up if half == 0 else down)
        for owner in (side_up, side_down, side_far):
            arrived(h, half, owner)

    def load_queries(h, _):
        for g in range(GROUP):
            cols = pl.ds(pl.multiple_of((h * GROUP + g) * HD, HD), HD)
            x = q_ref[:, cols].astype(f32) + bias_ref[pl.ds(h * GROUP + g, 1), :]
            q_s[h, g * tokens : (g + 1) * tokens, :] = (x * cosine + turn(x) * sine).astype(bf16)
            do_s[h, g * tokens : (g + 1) * tokens, :] = do_ref[:, cols]
        return 0

    send_own(0)
    lax.fori_loop(0, KV, load_queries, 0)
    relay_near(0)
    send_own(1)

    row = lax.broadcasted_iota(jnp.int32, (tokens, keys), 0)
    col = lax.broadcasted_iota(jnp.int32, (tokens, keys), 1)
    mask_ref[0] = jnp.where(col < start_ref[0], 0.0, -1e30)
    mask_ref[1] = jnp.where(col <= row + me * tokens, 0.0, -1e30)

    def more_tables(i, _):
        table(lax.rem(me + i, n))
        return 0

    relay_far(0)
    lax.fori_loop(1, n, more_tables, 0)

    def finish(h):
        cols = pl.ds(pl.multiple_of(h * HD, HD), HD)

        def gather(source, total):
            r_copy(h, source, source).wait_recv()
            return total + rrecv[h, :, source].astype(f32)

        total = lax.fori_loop(me + 1, n, gather, rsend[h, :, me].astype(f32))
        gk_ref[:, cols] = (total[0] * cosine - turn(total[0]) * sine).astype(bf16)
        gv_ref[:, cols] = total[1].astype(bf16)

    def head(h, _):
        await_half(h, 0)
        q_t[...] = q_s[h].T
        stat[...] = jnp.full(stat.shape, -3e38, f32)

        def score(part, _):
            s = dot(q_s[h], kv[h, 0, part].reshape(keys, HD), 1, 1)
            s = (s.reshape(GROUP, tokens, keys) + mask_ref[part][None]).reshape(rows, keys)
            s_ref[part] = s
            m = stat[...]
            for t in range(keys // HD):
                m = jnp.maximum(m, s[:, t * HD : (t + 1) * HD])
            stat[...] = m
            return 0

        lax.fori_loop(0, 2, score, 0)

        @pl.when(h + 1 < KV)
        def _():
            relay_near(h + 1)

        stat[...] = jnp.broadcast_to(jnp.max(stat[...], axis=1, keepdims=True), stat.shape)
        norm[...] = jnp.zeros(norm.shape, f32)
        acc[...] = jnp.zeros(acc.shape, f32)
        await_half(h, 1)

        def weigh(part, _):
            m = stat[...]
            pieces = [
                jnp.exp2((s_ref[part, :, t * HD : (t + 1) * HD] - m) * EXP2_SCALE)
                for t in range(keys // HD)
            ]
            norm[...] += functools.reduce(lambda a, b: a + b, pieces)
            p = jnp.concatenate([x.astype(bf16) for x in pieces], axis=1)
            p_ref[part] = p
            acc[...] += dot(p, kv[h, 1, part].reshape(keys, HD), 1, 0)
            return 0

        lax.fori_loop(0, 2, weigh, 0)

        @pl.when(h + 1 < KV)
        def _():
            relay_far(h + 1)

        @pl.when(h + 2 < KV)
        def _():
            send_own(h + 2)

        inverse = 1.0 / jnp.sum(norm[...], axis=1, keepdims=True)
        out = (acc[...] * inverse).astype(bf16)
        for g in range(GROUP):
            cols = pl.ds(pl.multiple_of((h * GROUP + g) * HD, HD), HD)
            out_ref[:, cols] = out[g * tokens : (g + 1) * tokens]
        scaled = (do_s[h].astype(f32) * inverse).astype(bf16)
        do_n[...] = scaled
        do_t[...] = scaled.T
        delta = jnp.sum(scaled.astype(f32) * out.astype(f32), axis=1, keepdims=True)
        stat[...] = jnp.broadcast_to(delta, stat.shape)
        acc[...] = jnp.zeros(acc.shape, f32)

        def score_grad(part):
            dp = dot(do_n[...], kv[h, 1, part].reshape(keys, HD), 1, 1)
            delta = stat[...]
            ds = jnp.concatenate(
                [
                    (
                        (dp[:, t * HD : (t + 1) * HD] - delta)
                        * p_ref[part, :, t * HD : (t + 1) * HD].astype(f32)
                    ).astype(bf16)
                    for t in range(keys // HD)
                ],
                axis=1,
            )
            acc[...] += dot(ds, kv[h, 0, part].reshape(keys, HD), 1, 0)
            return ds

        ds = score_grad(1)
        dk = dot(q_t[...], ds, 1, 0).T * SCALE
        dv = dot(do_t[...], p_ref[1], 1, 0).T
        rsend[h, 0] = dk.astype(bf16).reshape(n, tokens, HD)
        rsend[h, 1] = dv.astype(bf16).reshape(n, tokens, HD)

        def send_back(peer, _):
            r_copy(h, me, peer).start()
            return 0

        lax.fori_loop(0, me, send_back, 0)
        gk = dk * cos_s[...] - turn(dk) * sin_s[...]
        sum_a[me, pl.ds(HQ + h, 1), :] = jnp.sum(gk, axis=0, keepdims=True)
        sum_a[me, pl.ds(HQ + KV + h, 1), :] = jnp.sum(dv, axis=0, keepdims=True)
        score_grad(0)
        dq = (acc[...] * SCALE).astype(bf16).astype(f32)
        sums = []
        for g in range(GROUP):
            cols = pl.ds(pl.multiple_of((h * GROUP + g) * HD, HD), HD)
            x = dq[g * tokens : (g + 1) * tokens]
            gq = x * cosine - turn(x) * sine
            gq_ref[:, cols] = gq.astype(bf16)
            sums.append(jnp.sum(gq, axis=0, keepdims=True))
        sum_a[me, pl.ds(pl.multiple_of(h * GROUP, GROUP), GROUP), :] = jnp.concatenate(sums, axis=0)

        @pl.when(h > 0)
        def _():
            finish(h - 1)

        return 0

    lax.fori_loop(0, KV, head, 0)

    def exchange(size, index, device, buffer, send, recv):
        def copy(owner, peer):
            return pltpu.make_async_remote_copy(
                src_ref=buffer.at[owner], dst_ref=buffer.at[owner], send_sem=send.at[peer], recv_sem=recv.at[owner],
                device_id=device(peer), device_id_type=MESH,
            )

        def begin(i, _):
            copy(index, lax.rem(index + i, size)).start()
            return 0

        def arrive(i, _):
            peer = lax.rem(index + i, size)
            copy(peer, peer).wait_recv()
            return 0

        def leave(i, _):
            copy(index, lax.rem(index + i, size)).wait_send()
            return 0

        lax.fori_loop(1, size, begin, 0)
        return (
            lambda: lax.fori_loop(1, size, arrive, 0),
            lambda: lax.fori_loop(1, size, leave, 0),
        )

    arrive_a, leave_a = exchange(n, me, lambda p: {"seq": p}, sum_a, a_send, a_recv)
    finish(KV - 1)
    arrive_a()
    sum_b[lane] = jnp.sum(sum_a[...], axis=0)
    arrive_b, leave_b = exchange(inner, lane, lambda p: {"dp": block * inner + p}, sum_b, b_send, b_recv)
    arrive_b()
    sum_c[block] = jnp.sum(sum_b[...], axis=0)
    arrive_c, leave_c = exchange(outer, block, lambda p: {"dp": p * inner + lane}, sum_c, c_send, c_recv)

    def drain_head(h, _):
        for half in range(2):
            for slot, peer in enumerate((side, up, down, up, down, up if half == 0 else down, side)):
                kv_copy(h, half, me, peer, slot).wait_send()

        def drain_r(peer, _):
            r_copy(h, me, peer).wait_send()
            return 0

        return lax.fori_loop(0, me, drain_r, 0)

    lax.fori_loop(0, KV, drain_head, 0)
    leave_a()
    leave_b()
    arrive_c()
    sums_ref[...] = jnp.sum(sum_c[...], axis=0)
    leave_c()


def body(n, m, q_proj, k_proj, v_proj, cache_k, cache_v, bias_q, bias_k, bias_v, start, dout):
    tokens = q_proj.shape[1]
    keys, rows = n * tokens, GROUP * tokens
    inner = 8
    outer = m // inner
    half = HD // 2
    freqs = np.exp(-(2.0 * np.arange(half) / HD) * np.log(1e6)).astype(np.float32)
    freqs = jnp.asarray(np.concatenate([freqs, freqs])[None])
    bias = jnp.concatenate([bias_q, bias_k, bias_v]).astype(f32).reshape(SUMS, HD)
    vmem = pl.BlockSpec(memory_space=pltpu.VMEM)
    dma = pltpu.SemaphoreType.DMA
    out, grad_q, grad_k, grad_v, total = pl.pallas_call(
        functools.partial(attend_kernel, n, inner, outer),
        out_shape=[
            jax.ShapeDtypeStruct((tokens, HQ * HD), bf16),
            jax.ShapeDtypeStruct((tokens, HQ * HD), bf16),
            jax.ShapeDtypeStruct((tokens, KV * HD), bf16),
            jax.ShapeDtypeStruct((tokens, KV * HD), bf16),
            jax.ShapeDtypeStruct((SUMS, HD), f32),
        ],
        in_specs=[pl.BlockSpec(memory_space=pltpu.SMEM)] + [vmem] * 8,
        out_specs=[vmem] * 5,
        scratch_shapes=[
            pltpu.VMEM((KV, 2, 2, n, tokens, HD), bf16),
            pltpu.VMEM((KV, 2, n, tokens, HD), bf16),
            pltpu.VMEM((KV, 2, n, tokens, HD), bf16),
            pltpu.VMEM((KV, rows, HD), bf16),
            pltpu.VMEM((KV, rows, HD), bf16),
            pltpu.VMEM((2, rows, keys), f32),
            pltpu.VMEM((2, rows, keys), bf16),
            pltpu.VMEM((2, tokens, keys), f32),
            pltpu.VMEM((rows, HD), f32),
            pltpu.VMEM((rows, HD), f32),
            pltpu.VMEM((rows, HD), f32),
            pltpu.VMEM((HD, rows), bf16),
            pltpu.VMEM((HD, rows), bf16),
            pltpu.VMEM((rows, HD), bf16),
            pltpu.VMEM((keys, HD), f32),
            pltpu.VMEM((keys, HD), f32),
            pltpu.VMEM((n, SUMS, HD), f32),
            pltpu.VMEM((inner, SUMS, HD), f32),
            pltpu.VMEM((outer, SUMS, HD), f32),
            dma((KV, 2, 7)),
            dma((KV, 2, n)),
            dma((KV, n)),
            dma((KV, n)),
            dma((n,)),
            dma((n,)),
            dma((inner,)),
            dma((inner,)),
            dma((outer,)),
            dma((outer,)),
        ],
        compiler_params=pltpu.CompilerParams(collective_id=0, has_side_effects=True, vmem_limit_bytes=VMEM_LIMIT),
        name="attend",
    )(start, bias, freqs, q_proj[0], k_proj[0], v_proj[0], cache_k[0], cache_v[0], dout[0])
    total = total.reshape(SUMS * HD)
    split = HQ * HD
    return (
        out[None], grad_q[None], grad_k[None], grad_v[None],
        total[:split], total[split : split + KV * HD], total[split + KV * HD :],
    )


VMEM_LIMIT = 44 << 20


def solution(mesh):
    n, m = mesh.shape["seq"], mesh.shape["dp"]
    tokens = P("dp", "seq", None)
    return jax.shard_map(
        functools.partial(body, n, m),
        mesh=mesh,
        in_specs=(tokens, tokens, tokens, tokens, tokens, P(), P(), P(), P("dp"), tokens),
        out_specs=(tokens, tokens, tokens, tokens, P(), P(), P()),
        check_vma=False,
    )
```

```python
import functools

import jax
import jax.numpy as jnp
import numpy as np
from jax import lax
from jax.experimental import pallas as pl
from jax.experimental.pallas import tpu as pltpu
from jax.sharding import PartitionSpec as P

HQ = 32
KV = 4
HD = 128
GROUP = 8
SUMS = HQ + 2 * KV
SLOTS = 16
SCALE = float(HD**-0.5)
EXP2_SCALE = float(np.log2(np.e) * HD**-0.5)
MESH = pl.DeviceIdType.MESH
f32 = jnp.float32
bf16 = jnp.bfloat16


def dot(a, b, contract_a, contract_b):
    return lax.dot_general(
        a, b, (((contract_a,), (contract_b,)), ((), ())), preferred_element_type=f32
    )


def turn(x):
    return pltpu.roll(x, HD // 2, axis=1)


def attend_kernel(
    n, inner, outer,
    start_ref, bias_ref, freq_ref, q_ref, k_ref, v_ref, ck_ref, cv_ref, do_ref,
    out_ref, gq_ref, gk_ref, gv_ref, sums_ref,
    q_in, k_in, v_in, kv, rsend, rrecv, q_s, do_s, s_ref, p_ref, mask_ref, stat, norm, acc, q_t, do_t, do_n,
    cos_s, sin_s, sum_a, sum_b, sum_c,
    in_sem, cache_sem, do_sem, kv_send, kv_recv, r_send, r_recv,
    a_send, a_recv, b_send, b_recv, c_send, c_recv,
):
    me, mine = lax.axis_index("seq"), lax.axis_index("dp")
    tokens = q_ref.shape[0]
    keys = n * tokens
    rows = GROUP * tokens
    ring = n // 2
    y, z = me // 2, lax.rem(me, 2)

    def place(dy, dz):
        return lax.rem(y + dy, ring) * 2 + lax.rem(z + dz, 2)

    up, down, far = place(1, 0), place(ring - 1, 0), place(2, 0)
    side, side_up, side_down, side_far = place(0, 1), place(1, 1), place(ring - 1, 1), place(2, 1)
    block, lane = mine // inner, lax.rem(mine, inner)

    def head_cols(h):
        return pl.ds(pl.multiple_of(h * HD, HD), HD)

    fetch_k = pltpu.make_async_copy(k_ref, k_in, in_sem.at[0])
    fetch_v = pltpu.make_async_copy(v_ref, v_in, in_sem.at[1])
    fetch_q = pltpu.make_async_copy(q_ref, q_in, in_sem.at[2])

    def fetch_cache(h, half):
        source = (ck_ref, cv_ref)[half]
        return pltpu.make_async_copy(source.at[:, head_cols(h)], kv.at[h, half, 0, me], cache_sem.at[h, half])

    def fetch_do(h, g):
        target = do_s.at[h, pl.ds(pl.multiple_of(g * tokens, tokens), tokens), :]
        return pltpu.make_async_copy(do_ref.at[:, head_cols(h * GROUP + g)], target, do_sem.at[h, g])

    fetch_k.start()
    fetch_v.start()

    def begin_cache(h, _):
        fetch_cache(h, 0).start()
        fetch_cache(h, 1).start()
        return 0

    lax.fori_loop(0, KV, begin_cache, 0)
    fetch_q.start()

    barrier = pltpu.get_barrier_semaphore()

    def greet(device):
        pl.semaphore_signal(barrier, inc=1, device_id=device, device_id_type=MESH)

    def greet_seq(i, _):
        greet({"seq": lax.rem(me + i, n)})
        return 0

    def greet_inner(i, _):
        greet({"dp": block * inner + lax.rem(lane + i, inner)})
        return 0

    def greet_outer(i, _):
        greet({"dp": lax.rem(block + i, outer) * inner + lane})
        return 0

    lax.fori_loop(1, n, greet_seq, 0)
    lax.fori_loop(1, inner, greet_inner, 0)
    lax.fori_loop(1, outer, greet_outer, 0)

    flip = jnp.where(lax.broadcasted_iota(jnp.int32, (1, HD), 1) < HD // 2, -1.0, 1.0)

    def table(owner):
        at = pl.ds(pl.multiple_of(owner * tokens, tokens), tokens)
        position = start_ref[0] + owner * tokens + lax.broadcasted_iota(jnp.int32, (tokens, HD), 0)
        angle = position.astype(f32) * freq_ref[...]
        cos_s[at, :] = jnp.cos(angle)
        sin_s[at, :] = jnp.sin(angle) * flip

    table(me)
    own_rows = pl.ds(pl.multiple_of(me * tokens, tokens), tokens)
    cosine, sine = cos_s[own_rows, :], sin_s[own_rows, :]
    fetch_k.wait()
    fetch_v.wait()
    for h in range(KV):
        cols = slice(h * HD, (h + 1) * HD)
        x = k_in[:, cols].astype(f32) + bias_ref[HQ + h : HQ + h + 1, :]
        kv[h, 0, 1, me] = (x * cosine + turn(x) * sine).astype(bf16)
        kv[h, 1, 1, me] = (v_in[:, cols].astype(f32) + bias_ref[HQ + KV + h : HQ + KV + h + 1, :]).astype(bf16)

    pl.semaphore_wait(barrier, n + inner + outer - 3)

    def kv_copy(h, part, owner, peer, slot):
        block = kv.at[h, :, part, owner]
        return pltpu.make_async_remote_copy(
            src_ref=block, dst_ref=block,
            send_sem=kv_send.at[h, part, slot], recv_sem=kv_recv.at[h, part, owner],
            device_id={"seq": peer}, device_id_type=MESH,
        )

    top = ring - 1
    routes = (
        (me, side, jnp.logical_or(z == 0, y < top)),
        (me, up, y < top),
        (me, down, y == 0),
        (side, up, y < top),
        (side, down, y <= 1),
        (down, up, jnp.logical_and(y >= 1, y < top)),
        (side_up, down, jnp.logical_or(y == 0, y == top)),
    )

    def both_parts(needed, step):
        step(0)

        @pl.when(needed)
        def _():
            step(1)

    def send(h, *slots):
        for slot in slots:
            owner, peer, needed = routes[slot]
            both_parts(needed, lambda part: kv_copy(h, part, owner, peer, slot).start())

    def arrived(h, owner, needed):
        both_parts(needed, lambda part: kv_copy(h, part, owner, owner, 0).wait_recv())

    def send_own(h):
        send(h, 0, 1, 2)

    def relay_near(h):
        arrived(h, side, jnp.logical_or(z == 1, y < top))
        send(h, 3, 4)
        arrived(h, down, y >= 1)
        send(h, 5)

    def relay_far(h):
        arrived(h, side_up, jnp.logical_or(y == top, y == 0))
        send(h, 6)

    def await_rest(h):
        arrived(h, up, y == top)
        arrived(h, side_down, y >= 1)
        arrived(h, far, y >= 2)
        arrived(h, side_far, y >= 2)

    def direct(step):
        for part in range(2):

            def one(i, _):
                peer = lax.rem(me + i, n)
                pl.when(jnp.logical_or(part == 0, peer > me))(lambda: step(kv_copy(0, part, me, peer, i - 1)))
                return 0

            lax.fori_loop(1, n, one, 0)

    def await_direct():
        def one(i, _):
            owner = lax.rem(me + i, n)
            arrived(0, owner, owner < me)
            return 0

        lax.fori_loop(1, n, one, 0)

    def r_copy(h, source, peer):
        return pltpu.make_async_remote_copy(
            src_ref=rsend.at[h, peer], dst_ref=rrecv.at[h, source],
            send_sem=r_send.at[h, peer], recv_sem=r_recv.at[h, source],
            device_id={"seq": peer}, device_id_type=MESH,
        )

    def load_queries(h, _):
        for g in range(GROUP):
            cols = pl.ds(pl.multiple_of((h * GROUP + g) * HD, HD), HD)
            x = q_in[:, cols].astype(f32) + bias_ref[pl.ds(h * GROUP + g, 1), :]
            q_s[h, g * tokens : (g + 1) * tokens, :] = (x * cosine + turn(x) * sine).astype(bf16)
        return 0

    def await_cache(h, _):
        fetch_cache(h, 0).wait()
        fetch_cache(h, 1).wait()
        return 0

    lax.fori_loop(0, KV, await_cache, 0)
    direct(lambda copy: copy.start())
    send_own(1)

    def begin_do(i, _):
        fetch_do(i // GROUP, lax.rem(i, GROUP)).start()
        return 0

    lax.fori_loop(0, KV * GROUP, begin_do, 0)
    fetch_q.wait()
    lax.fori_loop(0, KV, load_queries, 0)

    row = lax.broadcasted_iota(jnp.int32, (tokens, keys), 0)
    col = lax.broadcasted_iota(jnp.int32, (tokens, keys), 1)
    mask_ref[0] = jnp.where(col < start_ref[0], 0.0, -1e30)
    mask_ref[1] = jnp.where(col <= row + me * tokens, 0.0, -1e30)

    def more_tables(i, _):
        table(lax.rem(me + i, n))
        return 0

    lax.fori_loop(1, n, more_tables, 0)

    def finish(h):
        cols = pl.ds(pl.multiple_of(h * HD, HD), HD)

        def gather(source, total):
            r_copy(h, source, source).wait_recv()
            return total + rrecv[h, source].astype(f32)

        total = lax.fori_loop(me + 1, n, gather, rsend[h, me].astype(f32))
        gk_ref[:, cols] = (total[0] * cosine - turn(total[0]) * sine).astype(bf16)
        gv_ref[:, cols] = total[1].astype(bf16)

    early, late = slice(0, KV - 1), slice(KV - 1, KV)

    def exchange(size, index, device, buffer, send_sem, recv_sem):
        def copy(which, owner, peer):
            block = buffer.at[owner, (early, late)[which]]
            return pltpu.make_async_remote_copy(
                src_ref=block, dst_ref=block, send_sem=send_sem.at[which, peer], recv_sem=recv_sem.at[which, owner],
                device_id=device(peer), device_id_type=MESH,
            )

        def begin(which):
            def one(i, _):
                copy(which, index, lax.rem(index + i, size)).start()
                return 0

            lax.fori_loop(1, size, one, 0)

        def arrive(which):
            def one(i, _):
                peer = lax.rem(index + i, size)
                copy(which, peer, peer).wait_recv()
                return 0

            lax.fori_loop(1, size, one, 0)
            return jnp.sum(buffer[:, (early, late)[which]], axis=0)

        def leave(which):
            def one(i, _):
                copy(which, index, lax.rem(index + i, size)).wait_send()
                return 0

            lax.fori_loop(1, size, one, 0)

        return begin, arrive, leave

    begin_a, arrive_a, leave_a = exchange(n, me, lambda p: {"seq": p}, sum_a, a_send, a_recv)
    begin_b, arrive_b, leave_b = exchange(inner, lane, lambda p: {"dp": block * inner + p}, sum_b, b_send, b_recv)
    begin_c, arrive_c, leave_c = exchange(outer, block, lambda p: {"dp": p * inner + lane}, sum_c, c_send, c_recv)

    def head(h, _):
        last = h == KV - 1

        @pl.when(last)
        def _():
            begin_a(0)

        @pl.when(h == 0)
        def _():
            await_direct()

        @pl.when(h > 0)
        def _():
            await_rest(h)

        q_t[...] = q_s[h].T
        stat[...] = jnp.full(stat.shape, -3e38, f32)

        def score(part, _):
            s = dot(q_s[h], kv[h, 0, part].reshape(keys, HD), 1, 1)
            s = (s.reshape(GROUP, tokens, keys) + mask_ref[part][None]).reshape(rows, keys)
            s_ref[part] = s
            m = stat[...]
            for t in range(keys // HD):
                m = jnp.maximum(m, s[:, t * HD : (t + 1) * HD])
            stat[...] = m
            return 0

        lax.fori_loop(0, 2, score, 0)

        @pl.when(h + 1 < KV)
        def _():
            relay_near(h + 1)


        stat[...] = jnp.broadcast_to(jnp.max(stat[...], axis=1, keepdims=True), stat.shape)
        norm[...] = jnp.zeros(norm.shape, f32)
        acc[...] = jnp.zeros(acc.shape, f32)

        def weigh(part, _):
            m = stat[...]
            pieces = [
                jnp.exp2((s_ref[part, :, t * HD : (t + 1) * HD] - m) * EXP2_SCALE)
                for t in range(keys // HD)
            ]
            norm[...] += functools.reduce(lambda a, b: a + b, pieces)
            p = jnp.concatenate([x.astype(bf16) for x in pieces], axis=1)
            p_ref[part] = p
            acc[...] += dot(p, kv[h, 1, part].reshape(keys, HD), 1, 0)
            return 0

        lax.fori_loop(0, 2, weigh, 0)

        @pl.when(h + 1 < KV)
        def _():
            relay_far(h + 1)

        @pl.when(h + 2 < KV)
        def _():
            send_own(h + 2)

        @pl.when(last)
        def _():
            sum_b[lane, early] = arrive_a(0)
            begin_b(0)

        def await_do(g, _):
            fetch_do(h, g).wait()
            return 0

        lax.fori_loop(0, GROUP, await_do, 0)
        inverse = 1.0 / jnp.sum(norm[...], axis=1, keepdims=True)
        out = (acc[...] * inverse).astype(bf16)
        for g in range(GROUP):
            cols = pl.ds(pl.multiple_of((h * GROUP + g) * HD, HD), HD)
            out_ref[:, cols] = out[g * tokens : (g + 1) * tokens]
        scaled = (do_s[h].astype(f32) * inverse).astype(bf16)
        do_n[...] = scaled
        do_t[...] = scaled.T
        delta = jnp.sum(scaled.astype(f32) * out.astype(f32), axis=1, keepdims=True)
        stat[...] = jnp.broadcast_to(delta, stat.shape)
        acc[...] = jnp.zeros(acc.shape, f32)

        def score_grad(part):
            dp = dot(do_n[...], kv[h, 1, part].reshape(keys, HD), 1, 1)
            delta = stat[...]
            ds = jnp.concatenate(
                [
                    (
                        (dp[:, t * HD : (t + 1) * HD] - delta)
                        * p_ref[part, :, t * HD : (t + 1) * HD].astype(f32)
                    ).astype(bf16)
                    for t in range(keys // HD)
                ],
                axis=1,
            )
            acc[...] += dot(ds, kv[h, 0, part].reshape(keys, HD), 1, 0)
            return ds

        ds = score_grad(1)
        dk = dot(q_t[...], ds, 1, 0).T * SCALE
        dv = dot(do_t[...], p_ref[1], 1, 0).T
        for r in range(n):
            rsend[h, r, 0] = dk[r * tokens : (r + 1) * tokens].astype(bf16)
            rsend[h, r, 1] = dv[r * tokens : (r + 1) * tokens].astype(bf16)

        def send_back(peer, _):
            r_copy(h, me, peer).start()
            return 0

        lax.fori_loop(0, me, send_back, 0)
        gk = dk * cos_s[...] - turn(dk) * sin_s[...]
        key_sums = [jnp.sum(gk, axis=0, keepdims=True), jnp.sum(dv, axis=0, keepdims=True)]
        score_grad(0)
        dq = (acc[...] * SCALE).astype(bf16).astype(f32)
        sums = []
        for g in range(GROUP):
            cols = pl.ds(pl.multiple_of((h * GROUP + g) * HD, HD), HD)
            x = dq[g * tokens : (g + 1) * tokens]
            gq = x * cosine - turn(x) * sine
            gq_ref[:, cols] = gq.astype(bf16)
            sums.append(jnp.sum(gq, axis=0, keepdims=True))
        filler = jnp.zeros((SLOTS - GROUP - 2, HD), f32)
        sum_a[me, h] = jnp.concatenate(sums + key_sums + [filler], axis=0)

        @pl.when(h > 0)
        def _():
            finish(h - 1)

        return 0

    lax.fori_loop(0, KV, head, 0)

    begin_a(1)
    sum_c[block, early] = arrive_b(0)
    begin_c(0)
    sum_b[lane, late] = arrive_a(1)
    begin_b(1)
    finish(KV - 1)
    sum_c[block, late] = arrive_b(1)
    begin_c(1)

    def drain_head(h, _):
        for slot, (_owner, peer, needed) in enumerate(routes):
            both_parts(needed, lambda part: kv_copy(h, part, me, peer, slot).wait_send())
        return 0

    def drain_back(h, _):
        def one(peer, _):
            r_copy(h, me, peer).wait_send()
            return 0

        return lax.fori_loop(0, me, one, 0)

    direct(lambda copy: copy.wait_send())
    lax.fori_loop(1, KV, drain_head, 0)
    lax.fori_loop(0, KV, drain_back, 0)
    for which in range(2):
        leave_a(which)
        leave_b(which)
    sums_ref[early] = arrive_c(0)
    sums_ref[late] = arrive_c(1)
    leave_c(0)
    leave_c(1)


def body(n, m, q_proj, k_proj, v_proj, cache_k, cache_v, bias_q, bias_k, bias_v, start, dout):
    tokens = q_proj.shape[1]
    keys, rows = n * tokens, GROUP * tokens
    inner = 8
    outer = m // inner
    half = HD // 2
    freqs = np.exp(-(2.0 * np.arange(half) / HD) * np.log(1e6)).astype(np.float32)
    freqs = jnp.asarray(np.concatenate([freqs, freqs])[None])
    bias = jnp.concatenate([bias_q, bias_k, bias_v]).astype(f32).reshape(SUMS, HD)
    vmem = pl.BlockSpec(memory_space=pltpu.VMEM)
    dma = pltpu.SemaphoreType.DMA
    out, grad_q, grad_k, grad_v, total = pl.pallas_call(
        functools.partial(attend_kernel, n, inner, outer),
        out_shape=[
            jax.ShapeDtypeStruct((tokens, HQ * HD), bf16),
            jax.ShapeDtypeStruct((tokens, HQ * HD), bf16),
            jax.ShapeDtypeStruct((tokens, KV * HD), bf16),
            jax.ShapeDtypeStruct((tokens, KV * HD), bf16),
            jax.ShapeDtypeStruct((KV, SLOTS, HD), f32),
        ],
        in_specs=[pl.BlockSpec(memory_space=pltpu.SMEM), vmem, vmem] + [pl.BlockSpec(memory_space=pltpu.HBM)] * 6,
        out_specs=[vmem] * 5,
        scratch_shapes=[
            pltpu.VMEM((tokens, HQ * HD), bf16),
            pltpu.VMEM((tokens, KV * HD), bf16),
            pltpu.VMEM((tokens, KV * HD), bf16),
            pltpu.VMEM((KV, 2, 2, n, tokens, HD), bf16),
            pltpu.VMEM((KV, n, 2, tokens, HD), bf16),
            pltpu.VMEM((KV, n, 2, tokens, HD), bf16),
            pltpu.VMEM((KV, rows, HD), bf16),
            pltpu.VMEM((KV, rows, HD), bf16),
            pltpu.VMEM((2, rows, keys), f32),
            pltpu.VMEM((2, rows, keys), bf16),
            pltpu.VMEM((2, tokens, keys), f32),
            pltpu.VMEM((rows, HD), f32),
            pltpu.VMEM((rows, HD), f32),
            pltpu.VMEM((rows, HD), f32),
            pltpu.VMEM((HD, rows), bf16),
            pltpu.VMEM((HD, rows), bf16),
            pltpu.VMEM((rows, HD), bf16),
            pltpu.VMEM((keys, HD), f32),
            pltpu.VMEM((keys, HD), f32),
            pltpu.VMEM((n, KV, SLOTS, HD), f32),
            pltpu.VMEM((inner, KV, SLOTS, HD), f32),
            pltpu.VMEM((outer, KV, SLOTS, HD), f32),
            dma((3,)),
            dma((KV, 2)),
            dma((KV, GROUP)),
            dma((KV, 2, 7)),
            dma((KV, 2, n)),
            dma((KV, n)),
            dma((KV, n)),
            dma((2, n)),
            dma((2, n)),
            dma((2, inner)),
            dma((2, inner)),
            dma((2, outer)),
            dma((2, outer)),
        ],
        compiler_params=pltpu.CompilerParams(collective_id=0, has_side_effects=True, vmem_limit_bytes=VMEM_LIMIT),
        name="attend",
    )(start, bias, freqs, *(pltpu.with_memory_space_constraint(x[0], pltpu.HBM) for x in (q_proj, k_proj, v_proj, cache_k, cache_v, dout)))
    return (
        out[None], grad_q[None], grad_k[None], grad_v[None],
        total[:, :GROUP].reshape(HQ * HD), total[:, GROUP].reshape(KV * HD), total[:, GROUP + 1].reshape(KV * HD),
    )


VMEM_LIMIT = 44 << 20


def solution(mesh):
    n, m = mesh.shape["seq"], mesh.shape["dp"]
    tokens = P("dp", "seq", None)
    return jax.shard_map(
        functools.partial(body, n, m),
        mesh=mesh,
        in_specs=(tokens, tokens, tokens, tokens, tokens, P(), P(), P(), P("dp"), tokens),
        out_specs=(tokens, tokens, tokens, tokens, P(), P(), P()),
        check_vma=False,
    )
```

```python
import functools

import jax
import jax.numpy as jnp
import numpy as np
from jax import lax
from jax.experimental import pallas as pl
from jax.experimental.pallas import tpu as pltpu
from jax.sharding import PartitionSpec as P

HQ = 32
KV = 4
HD = 128
GROUP = 8
SUMS = HQ + 2 * KV
SLOTS = 16
LOG_BASE = float(np.log(1e6))
SCALE = float(HD**-0.5)
EXP2_SCALE = float(np.log2(np.e) * HD**-0.5)
MESH = pl.DeviceIdType.MESH
f32 = jnp.float32
bf16 = jnp.bfloat16


def dot(a, b, contract_a, contract_b):
    return lax.dot_general(
        a, b, (((contract_a,), (contract_b,)), ((), ())), preferred_element_type=f32
    )


def turn(x):
    return pltpu.roll(x, HD // 2, axis=1)


def attend_kernel(
    n, inner, outer,
    start_ref, bias_ref, q_ref, k_ref, v_ref, ck_ref, cv_ref, do_ref,
    out_ref, gq_ref, gk_ref, gv_ref, sums_ref,
    q_in, k_in, v_in, kv, rsend, rrecv, q_s, do_s, s_ref, p_ref, mask_ref, stat, norm, acc, q_t, do_t, do_n,
    cos_s, sin_s, sum_a, sum_b, sum_c,
    in_sem, cache_sem, do_sem, kv_send, kv_recv, r_send, r_recv,
    a_send, a_recv, b_send, b_recv, c_send, c_recv,
):
    me, mine = lax.axis_index("seq"), lax.axis_index("dp")
    tokens = q_ref.shape[0]
    keys = n * tokens
    rows = GROUP * tokens
    ring = n // 2
    y, z = me // 2, lax.rem(me, 2)

    def place(dy, dz):
        return lax.rem(y + dy, ring) * 2 + lax.rem(z + dz, 2)

    up, down, far = place(1, 0), place(ring - 1, 0), place(2, 0)
    side, side_up, side_down, side_far = place(0, 1), place(1, 1), place(ring - 1, 1), place(2, 1)
    block, lane = mine // inner, lax.rem(mine, inner)

    def head_cols(h):
        return pl.ds(pl.multiple_of(h * HD, HD), HD)

    fetch_k = pltpu.make_async_copy(k_ref, k_in, in_sem.at[0])
    fetch_v = pltpu.make_async_copy(v_ref, v_in, in_sem.at[1])
    fetch_q = pltpu.make_async_copy(q_ref, q_in, in_sem.at[2])

    def fetch_cache(h, half):
        source = (ck_ref, cv_ref)[half]
        return pltpu.make_async_copy(source.at[:, head_cols(h)], kv.at[h, half, 0, me], cache_sem.at[h, half])

    def fetch_do(h, g):
        target = do_s.at[h, pl.ds(pl.multiple_of(g * tokens, tokens), tokens), :]
        return pltpu.make_async_copy(do_ref.at[:, head_cols(h * GROUP + g)], target, do_sem.at[h, g])

    fetch_k.start()
    fetch_v.start()

    def begin_cache(h, _):
        fetch_cache(h, 0).start()
        fetch_cache(h, 1).start()
        return 0

    lax.fori_loop(0, KV, begin_cache, 0)
    fetch_q.start()

    barrier = pltpu.get_barrier_semaphore()

    def greet(device):
        pl.semaphore_signal(barrier, inc=1, device_id=device, device_id_type=MESH)

    def greet_seq(i, _):
        greet({"seq": lax.rem(me + i, n)})
        return 0

    def greet_inner(i, _):
        greet({"dp": block * inner + lax.rem(lane + i, inner)})
        return 0

    def greet_outer(i, _):
        greet({"dp": lax.rem(block + i, outer) * inner + lane})
        return 0

    lax.fori_loop(1, n, greet_seq, 0)
    lax.fori_loop(1, inner, greet_inner, 0)
    lax.fori_loop(1, outer, greet_outer, 0)

    flip = jnp.where(lax.broadcasted_iota(jnp.int32, (1, HD), 1) < HD // 2, -1.0, 1.0)

    pair = lax.rem(lax.broadcasted_iota(jnp.int32, (1, HD), 1), HD // 2).astype(f32)
    freqs = jnp.exp(-(2.0 * pair / HD) * LOG_BASE)

    def table(owner):
        at = pl.ds(pl.multiple_of(owner * tokens, tokens), tokens)
        position = start_ref[0] + owner * tokens + lax.broadcasted_iota(jnp.int32, (tokens, HD), 0)
        angle = position.astype(f32) * freqs
        cos_s[at, :] = jnp.cos(angle)
        sin_s[at, :] = jnp.sin(angle) * flip

    table(me)
    own_rows = pl.ds(pl.multiple_of(me * tokens, tokens), tokens)
    cosine, sine = cos_s[own_rows, :], sin_s[own_rows, :]
    fetch_k.wait()
    fetch_v.wait()
    for h in range(KV):
        cols = slice(h * HD, (h + 1) * HD)
        x = k_in[:, cols].astype(f32) + bias_ref[HQ + h : HQ + h + 1, :]
        kv[h, 0, 1, me] = (x * cosine + turn(x) * sine).astype(bf16)
        kv[h, 1, 1, me] = (v_in[:, cols].astype(f32) + bias_ref[HQ + KV + h : HQ + KV + h + 1, :]).astype(bf16)

    pl.semaphore_wait(barrier, n + inner + outer - 3)

    def kv_copy(h, half, part, owner, peer, slot):
        block = kv.at[h, half, part, owner]
        return pltpu.make_async_remote_copy(
            src_ref=block, dst_ref=block,
            send_sem=kv_send.at[h, half, part, slot], recv_sem=kv_recv.at[h, half, part, owner],
            device_id={"seq": peer}, device_id_type=MESH,
        )

    top = ring - 1
    to_side = jnp.logical_or(z == 0, y < top)
    to_up = y < top
    to_down = (y == 0, y <= 1)
    pass_far = (jnp.logical_and(y >= 1, y < top), jnp.logical_or(y == 0, y == top))
    from_side = jnp.logical_or(z == 1, y < top)
    from_down = y >= 1
    from_up = (y == top, jnp.logical_or(y == top, y == 0))
    from_far = y >= 2

    def both_parts(needed, step):
        step(0)

        @pl.when(needed)
        def _():
            step(1)

    def send(h, half, owner, peer, slot, needed):
        both_parts(needed, lambda part: kv_copy(h, half, part, owner, peer, slot).start())

    def sent(h, half, peer, slot, needed):
        both_parts(needed, lambda part: kv_copy(h, half, part, me, peer, slot).wait_send())

    def arrived(h, half, owner, needed):
        both_parts(needed, lambda part: kv_copy(h, half, part, owner, owner, 0).wait_recv())

    def send_own(h):
        for half in range(2):
            send(h, half, me, side, 0, to_side)
            send(h, half, me, up, 1, to_up)
            send(h, half, me, down, 2, to_down[half])

    def relay_near(h):
        for half in range(2):
            arrived(h, half, side, from_side)
            send(h, half, side, up, 3, to_up)
            send(h, half, side, down, 4, to_down[half])
            if half == 0:
                arrived(h, 0, down, from_down)
                send(h, 0, down, up, 5, pass_far[0])
            else:
                arrived(h, 1, up, from_up[1])
                send(h, 1, up, down, 5, pass_far[1])

    def relay_far(h):
        arrived(h, 0, side_down, from_down)
        send(h, 0, side_down, up, 6, pass_far[0])
        arrived(h, 1, side_up, from_up[1])
        send(h, 1, side_up, down, 6, pass_far[1])

    def await_half(h, half):
        if half == 0:
            arrived(h, 0, up, from_up[0])
            arrived(h, 0, side_up, from_up[0])
        else:
            arrived(h, 1, down, from_down)
            arrived(h, 1, side_down, from_down)
        arrived(h, half, far, from_far)
        arrived(h, half, side_far, from_far)

    def direct(step):
        for half in range(2):
            for part in range(2):

                def one(i, _):
                    peer = lax.rem(me + i, n)
                    pl.when(jnp.logical_or(part == 0, peer > me))(lambda: step(kv_copy(0, half, part, me, peer, i - 1)))
                    return 0

                lax.fori_loop(1, n, one, 0)

    def await_direct(half):
        def one(i, _):
            owner = lax.rem(me + i, n)
            arrived(0, half, owner, owner < me)
            return 0

        lax.fori_loop(1, n, one, 0)

    def r_copy(h, source, peer):
        return pltpu.make_async_remote_copy(
            src_ref=rsend.at[h, peer], dst_ref=rrecv.at[h, source],
            send_sem=r_send.at[h, peer], recv_sem=r_recv.at[h, source],
            device_id={"seq": peer}, device_id_type=MESH,
        )

    def load_queries(h, _):
        for g in range(GROUP):
            cols = pl.ds(pl.multiple_of((h * GROUP + g) * HD, HD), HD)
            x = q_in[:, cols].astype(f32) + bias_ref[pl.ds(h * GROUP + g, 1), :]
            q_s[h, g * tokens : (g + 1) * tokens, :] = (x * cosine + turn(x) * sine).astype(bf16)
        return 0

    def await_cache(h, _):
        fetch_cache(h, 0).wait()
        fetch_cache(h, 1).wait()
        return 0

    lax.fori_loop(0, KV, await_cache, 0)
    direct(lambda copy: copy.start())
    send_own(1)

    def begin_do(i, _):
        fetch_do(i // GROUP, lax.rem(i, GROUP)).start()
        return 0

    lax.fori_loop(0, KV * GROUP, begin_do, 0)
    fetch_q.wait()
    lax.fori_loop(0, KV, load_queries, 0)

    row = lax.broadcasted_iota(jnp.int32, (tokens, keys), 0)
    col = lax.broadcasted_iota(jnp.int32, (tokens, keys), 1)
    mask_ref[0] = jnp.where(col < start_ref[0], 0.0, -1e30)
    mask_ref[1] = jnp.where(col <= row + me * tokens, 0.0, -1e30)

    def more_tables(i, _):
        table(lax.rem(me + i, n))
        return 0

    lax.fori_loop(1, n, more_tables, 0)

    def finish(h):
        cols = pl.ds(pl.multiple_of(h * HD, HD), HD)

        def gather(source, total):
            r_copy(h, source, source).wait_recv()
            return total + rrecv[h, source].astype(f32)

        total = lax.fori_loop(me + 1, n, gather, rsend[h, me].astype(f32))
        gk_ref[:, cols] = (total[0] * cosine - turn(total[0]) * sine).astype(bf16)
        gv_ref[:, cols] = total[1].astype(bf16)

    early, late = slice(0, KV - 1), slice(KV - 1, KV)

    def exchange(size, index, device, buffer, send_sem, recv_sem):
        def copy(which, owner, peer):
            block = buffer.at[owner, (early, late)[which]]
            return pltpu.make_async_remote_copy(
                src_ref=block, dst_ref=block, send_sem=send_sem.at[which, peer], recv_sem=recv_sem.at[which, owner],
                device_id=device(peer), device_id_type=MESH,
            )

        def begin(which):
            def one(i, _):
                copy(which, index, lax.rem(index + i, size)).start()
                return 0

            lax.fori_loop(1, size, one, 0)

        def arrive(which):
            def one(i, _):
                peer = lax.rem(index + i, size)
                copy(which, peer, peer).wait_recv()
                return 0

            lax.fori_loop(1, size, one, 0)
            return jnp.sum(buffer[:, (early, late)[which]], axis=0)

        def leave(which):
            def one(i, _):
                copy(which, index, lax.rem(index + i, size)).wait_send()
                return 0

            lax.fori_loop(1, size, one, 0)

        return begin, arrive, leave

    begin_a, arrive_a, leave_a = exchange(n, me, lambda p: {"seq": p}, sum_a, a_send, a_recv)
    begin_b, arrive_b, leave_b = exchange(inner, lane, lambda p: {"dp": block * inner + p}, sum_b, b_send, b_recv)
    begin_c, arrive_c, leave_c = exchange(outer, block, lambda p: {"dp": p * inner + lane}, sum_c, c_send, c_recv)

    def head(h, _):
        last = h == KV - 1

        @pl.when(last)
        def _():
            begin_a(0)

        @pl.when(h == 0)
        def _():
            await_direct(0)

        @pl.when(h > 0)
        def _():
            await_half(h, 0)

        q_t[...] = q_s[h].T
        stat[...] = jnp.full(stat.shape, -3e38, f32)

        def score(part, _):
            s = dot(q_s[h], kv[h, 0, part].reshape(keys, HD), 1, 1)
            s = (s.reshape(GROUP, tokens, keys) + mask_ref[part][None]).reshape(rows, keys)
            s_ref[part] = s
            m = stat[...]
            for t in range(keys // HD):
                m = jnp.maximum(m, s[:, t * HD : (t + 1) * HD])
            stat[...] = m
            return 0

        for part in range(2):
            score(part, 0)

        @pl.when(h + 1 < KV)
        def _():
            relay_near(h + 1)


        stat[...] = jnp.broadcast_to(jnp.max(stat[...], axis=1, keepdims=True), stat.shape)
        norm[...] = jnp.zeros(norm.shape, f32)
        acc[...] = jnp.zeros(acc.shape, f32)

        @pl.when(h == 0)
        def _():
            await_direct(1)

        @pl.when(h > 0)
        def _():
            await_half(h, 1)


        def weigh(part, _):
            m = stat[...]
            pieces = [
                jnp.exp2((s_ref[part, :, t * HD : (t + 1) * HD] - m) * EXP2_SCALE)
                for t in range(keys // HD)
            ]
            norm[...] += functools.reduce(lambda a, b: a + b, pieces)
            p = jnp.concatenate([x.astype(bf16) for x in pieces], axis=1)
            p_ref[part] = p
            acc[...] += dot(p, kv[h, 1, part].reshape(keys, HD), 1, 0)
            return 0

        lax.fori_loop(0, 2, weigh, 0)

        @pl.when(h + 1 < KV)
        def _():
            relay_far(h + 1)

        @pl.when(h + 2 < KV)
        def _():
            send_own(h + 2)

        @pl.when(last)
        def _():
            sum_b[lane, early] = arrive_a(0)
            begin_b(0)

        def await_do(g, _):
            fetch_do(h, g).wait()
            return 0

        lax.fori_loop(0, GROUP, await_do, 0)
        inverse = 1.0 / jnp.sum(norm[...], axis=1, keepdims=True)
        out = (acc[...] * inverse).astype(bf16)
        for g in range(GROUP):
            cols = pl.ds(pl.multiple_of((h * GROUP + g) * HD, HD), HD)
            out_ref[:, cols] = out[g * tokens : (g + 1) * tokens]
        scaled = (do_s[h].astype(f32) * inverse).astype(bf16)
        do_n[...] = scaled
        do_t[...] = scaled.T
        delta = jnp.sum(scaled.astype(f32) * out.astype(f32), axis=1, keepdims=True)
        stat[...] = jnp.broadcast_to(delta, stat.shape)
        acc[...] = jnp.zeros(acc.shape, f32)

        def score_grad(part):
            dp = dot(do_n[...], kv[h, 1, part].reshape(keys, HD), 1, 1)
            delta = stat[...]
            ds = jnp.concatenate(
                [
                    (
                        (dp[:, t * HD : (t + 1) * HD] - delta)
                        * p_ref[part, :, t * HD : (t + 1) * HD].astype(f32)
                    ).astype(bf16)
                    for t in range(keys // HD)
                ],
                axis=1,
            )
            acc[...] += dot(ds, kv[h, 0, part].reshape(keys, HD), 1, 0)
            return ds

        ds = score_grad(1)
        dk = dot(q_t[...], ds, 1, 0).T * SCALE
        dv = dot(do_t[...], p_ref[1], 1, 0).T
        for r in range(n):
            rsend[h, r, 0] = dk[r * tokens : (r + 1) * tokens].astype(bf16)
            rsend[h, r, 1] = dv[r * tokens : (r + 1) * tokens].astype(bf16)

        def send_back(peer, _):
            r_copy(h, me, peer).start()
            return 0

        lax.fori_loop(0, me, send_back, 0)
        gk = dk * cos_s[...] - turn(dk) * sin_s[...]
        key_sums = [jnp.sum(gk, axis=0, keepdims=True), jnp.sum(dv, axis=0, keepdims=True)]
        score_grad(0)
        dq = (acc[...] * SCALE).astype(bf16).astype(f32)
        sums = []
        for g in range(GROUP):
            cols = pl.ds(pl.multiple_of((h * GROUP + g) * HD, HD), HD)
            x = dq[g * tokens : (g + 1) * tokens]
            gq = x * cosine - turn(x) * sine
            gq_ref[:, cols] = gq.astype(bf16)
            sums.append(jnp.sum(gq, axis=0, keepdims=True))
        filler = jnp.zeros((SLOTS - GROUP - 2, HD), f32)
        sum_a[me, h] = jnp.concatenate(sums + key_sums + [filler], axis=0)

        @pl.when(h > 0)
        def _():
            finish(h - 1)

        return 0

    lax.fori_loop(0, KV, head, 0)

    begin_a(1)
    sum_c[block, early] = arrive_b(0)
    begin_c(0)
    sum_b[lane, late] = arrive_a(1)
    begin_b(1)
    finish(KV - 1)
    sum_c[block, late] = arrive_b(1)
    begin_c(1)

    def drain_head(h, _):
        for half in range(2):
            for slot, (peer, needed) in enumerate(
                (
                    (side, to_side), (up, to_up), (down, to_down[half]), (up, to_up), (down, to_down[half]),
                    (up if half == 0 else down, pass_far[half]), (up if half == 0 else down, pass_far[half]),
                )
            ):
                sent(h, half, peer, slot, needed)

        return 0

    def drain_back(h, _):
        def one(peer, _):
            r_copy(h, me, peer).wait_send()
            return 0

        return lax.fori_loop(0, me, one, 0)

    direct(lambda copy: copy.wait_send())
    lax.fori_loop(1, KV, drain_head, 0)
    lax.fori_loop(0, KV, drain_back, 0)
    for which in range(2):
        leave_a(which)
        leave_b(which)
    sums_ref[early] = arrive_c(0)
    sums_ref[late] = arrive_c(1)
    leave_c(0)
    leave_c(1)


def store_kernel(*refs):
    count = len(refs) // 2
    sources, targets, sem = refs[:count], refs[count : 2 * count], refs[-1]
    copies = [pltpu.make_async_copy(a, b, sem.at[i]) for i, (a, b) in enumerate(zip(sources, targets))]
    for copy in copies:
        copy.start()
    for copy in copies:
        copy.wait()


def body(n, m, q_proj, k_proj, v_proj, cache_k, cache_v, bias_q, bias_k, bias_v, start, dout):
    tokens = q_proj.shape[1]
    keys, rows = n * tokens, GROUP * tokens
    inner = 8
    outer = m // inner
    bias = jnp.concatenate([bias_q, bias_k, bias_v]).astype(f32).reshape(SUMS, HD)
    vmem = pl.BlockSpec(memory_space=pltpu.VMEM)
    dma = pltpu.SemaphoreType.DMA
    out, grad_q, grad_k, grad_v, total = pl.pallas_call(
        functools.partial(attend_kernel, n, inner, outer),
        out_shape=[
            jax.ShapeDtypeStruct((tokens, HQ * HD), bf16),
            jax.ShapeDtypeStruct((tokens, HQ * HD), bf16),
            jax.ShapeDtypeStruct((tokens, KV * HD), bf16),
            jax.ShapeDtypeStruct((tokens, KV * HD), bf16),
            jax.ShapeDtypeStruct((KV, SLOTS, HD), f32),
        ],
        in_specs=[pl.BlockSpec(memory_space=pltpu.SMEM), vmem] + [pl.BlockSpec(memory_space=pltpu.HBM)] * 6,
        out_specs=[vmem] * 5,
        scratch_shapes=[
            pltpu.VMEM((tokens, HQ * HD), bf16),
            pltpu.VMEM((tokens, KV * HD), bf16),
            pltpu.VMEM((tokens, KV * HD), bf16),
            pltpu.VMEM((KV, 2, 2, n, tokens, HD), bf16),
            pltpu.VMEM((KV, n, 2, tokens, HD), bf16),
            pltpu.VMEM((KV, n, 2, tokens, HD), bf16),
            pltpu.VMEM((KV, rows, HD), bf16),
            pltpu.VMEM((KV, rows, HD), bf16),
            pltpu.VMEM((2, rows, keys), f32),
            pltpu.VMEM((2, rows, keys), bf16),
            pltpu.VMEM((2, tokens, keys), f32),
            pltpu.VMEM((rows, HD), f32),
            pltpu.VMEM((rows, HD), f32),
            pltpu.VMEM((rows, HD), f32),
            pltpu.VMEM((HD, rows), bf16),
            pltpu.VMEM((HD, rows), bf16),
            pltpu.VMEM((rows, HD), bf16),
            pltpu.VMEM((keys, HD), f32),
            pltpu.VMEM((keys, HD), f32),
            pltpu.VMEM((n, KV, SLOTS, HD), f32),
            pltpu.VMEM((inner, KV, SLOTS, HD), f32),
            pltpu.VMEM((outer, KV, SLOTS, HD), f32),
            dma((3,)),
            dma((KV, 2)),
            dma((KV, GROUP)),
            dma((KV, 2, 2, 7)),
            dma((KV, 2, 2, n)),
            dma((KV, n)),
            dma((KV, n)),
            dma((2, n)),
            dma((2, n)),
            dma((2, inner)),
            dma((2, inner)),
            dma((2, outer)),
            dma((2, outer)),
        ],
        compiler_params=pltpu.CompilerParams(collective_id=0, has_side_effects=True, vmem_limit_bytes=VMEM_LIMIT),
        name="attend",
    )(start, bias, *(pltpu.with_memory_space_constraint(x[0], pltpu.HBM) for x in (q_proj, k_proj, v_proj, cache_k, cache_v, dout)))
    anywhere, hbm = pl.BlockSpec(memory_space=pl.ANY), pl.BlockSpec(memory_space=pltpu.HBM)
    results = pl.pallas_call(
        store_kernel,
        out_shape=[jax.ShapeDtypeStruct(x.shape, x.dtype) for x in (out, grad_q, grad_k, grad_v)],
        in_specs=[anywhere] * 4,
        out_specs=[hbm] * 4,
        scratch_shapes=[dma((4,))],
        compiler_params=pltpu.CompilerParams(vmem_limit_bytes=1 << 20),
        name="store",
    )(out, grad_q, grad_k, grad_v)
    return (
        *(x[None] for x in results),
        total[:, :GROUP].reshape(HQ * HD), total[:, GROUP].reshape(KV * HD), total[:, GROUP + 1].reshape(KV * HD),
    )


VMEM_LIMIT = 44 << 20


def solution(mesh):
    n, m = mesh.shape["seq"], mesh.shape["dp"]
    tokens = P("dp", "seq", None)
    return jax.shard_map(
        functools.partial(body, n, m),
        mesh=mesh,
        in_specs=(tokens, tokens, tokens, tokens, tokens, P(), P(), P(), P("dp"), tokens),
        out_specs=(tokens, tokens, tokens, tokens, P(), P(), P()),
        check_vma=False,
    )
```

```python
import functools

import jax
import jax.numpy as jnp
import numpy as np
from jax import lax
from jax.experimental import pallas as pl
from jax.experimental.pallas import tpu as pltpu
from jax.sharding import PartitionSpec as P

HQ = 32
KV = 4
HD = 128
GROUP = 8
SUMS = HQ + 2 * KV
SLOTS = 16
LOG_BASE = float(np.log(1e6))
SCALE = float(HD**-0.5)
EXP2_SCALE = float(np.log2(np.e) * HD**-0.5)
MESH = pl.DeviceIdType.MESH
f32 = jnp.float32
bf16 = jnp.bfloat16


def dot(a, b, contract_a, contract_b):
    return lax.dot_general(
        a, b, (((contract_a,), (contract_b,)), ((), ())), preferred_element_type=f32
    )


def turn(x):
    return pltpu.roll(x, HD // 2, axis=1)


def attend_kernel(
    n, inner, outer,
    start_ref, bias_ref, q_ref, k_ref, v_ref, ck_ref, cv_ref, do_ref,
    out_ref, gq_ref, gk_ref, gv_ref, sums_ref,
    q_in, k_in, v_in, kv, rsend, rrecv, q_s, do_s, s_ref, p_ref, mask_ref, stat, norm, acc, q_t, do_t, do_n,
    cos_s, sin_s, sum_a, sum_b, sum_c,
    in_sem, cache_sem, do_sem, kv_send, kv_recv, r_send, r_recv,
    a_send, a_recv, b_send, b_recv, c_send, c_recv,
):
    me, mine = lax.axis_index("seq"), lax.axis_index("dp")
    tokens = q_ref.shape[0]
    keys = n * tokens
    rows = GROUP * tokens
    ring = n // 2
    y, z = me // 2, lax.rem(me, 2)

    def place(dy, dz):
        return lax.rem(y + dy, ring) * 2 + lax.rem(z + dz, 2)

    up, down, far = place(1, 0), place(ring - 1, 0), place(2, 0)
    side, side_up, side_down, side_far = place(0, 1), place(1, 1), place(ring - 1, 1), place(2, 1)
    block, lane = mine // inner, lax.rem(mine, inner)

    def head_cols(h):
        return pl.ds(pl.multiple_of(h * HD, HD), HD)

    fetch_k = pltpu.make_async_copy(k_ref, k_in, in_sem.at[0])
    fetch_v = pltpu.make_async_copy(v_ref, v_in, in_sem.at[1])
    fetch_q = pltpu.make_async_copy(q_ref, q_in, in_sem.at[2])

    def fetch_cache(h, half):
        source = (ck_ref, cv_ref)[half]
        return pltpu.make_async_copy(source.at[:, head_cols(h)], kv.at[h, half, 0, me], cache_sem.at[h, half])

    def fetch_do(h, g):
        target = do_s.at[h, pl.ds(pl.multiple_of(g * tokens, tokens), tokens), :]
        return pltpu.make_async_copy(do_ref.at[:, head_cols(h * GROUP + g)], target, do_sem.at[h, g])

    fetch_k.start()
    fetch_v.start()

    def begin_cache(h, _):
        fetch_cache(h, 0).start()
        fetch_cache(h, 1).start()
        return 0

    lax.fori_loop(0, KV, begin_cache, 0)
    fetch_q.start()

    barrier = pltpu.get_barrier_semaphore()

    def greet(device):
        pl.semaphore_signal(barrier, inc=1, device_id=device, device_id_type=MESH)

    def greet_seq(i, _):
        greet({"seq": lax.rem(me + i, n)})
        return 0

    def greet_inner(i, _):
        greet({"dp": block * inner + lax.rem(lane + i, inner)})
        return 0

    def greet_outer(i, _):
        greet({"dp": lax.rem(block + i, outer) * inner + lane})
        return 0

    lax.fori_loop(1, n, greet_seq, 0)
    lax.fori_loop(1, inner, greet_inner, 0)
    lax.fori_loop(1, outer, greet_outer, 0)

    flip = jnp.where(lax.broadcasted_iota(jnp.int32, (1, HD), 1) < HD // 2, -1.0, 1.0)

    pair = lax.rem(lax.broadcasted_iota(jnp.int32, (1, HD), 1), HD // 2).astype(f32)
    freqs = jnp.exp(-(2.0 * pair / HD) * LOG_BASE)

    def table(owner):
        at = pl.ds(pl.multiple_of(owner * tokens, tokens), tokens)
        position = start_ref[0] + owner * tokens + lax.broadcasted_iota(jnp.int32, (tokens, HD), 0)
        angle = position.astype(f32) * freqs
        cos_s[at, :] = jnp.cos(angle)
        sin_s[at, :] = jnp.sin(angle) * flip

    table(me)
    own_rows = pl.ds(pl.multiple_of(me * tokens, tokens), tokens)
    cosine, sine = cos_s[own_rows, :], sin_s[own_rows, :]
    fetch_k.wait()
    fetch_v.wait()
    for h in range(KV):
        cols = slice(h * HD, (h + 1) * HD)
        x = k_in[:, cols].astype(f32) + bias_ref[HQ + h : HQ + h + 1, :]
        kv[h, 0, 1, me] = (x * cosine + turn(x) * sine).astype(bf16)
        kv[h, 1, 1, me] = (v_in[:, cols].astype(f32) + bias_ref[HQ + KV + h : HQ + KV + h + 1, :]).astype(bf16)

    pl.semaphore_wait(barrier, n + inner + outer - 3)

    def kv_copy(h, half, part, owner, peer, slot):
        block = kv.at[h, half, part, owner]
        return pltpu.make_async_remote_copy(
            src_ref=block, dst_ref=block,
            send_sem=kv_send.at[h, half, part, slot], recv_sem=kv_recv.at[h, half, part, owner],
            device_id={"seq": peer}, device_id_type=MESH,
        )

    top = ring - 1
    to_side = jnp.logical_or(z == 0, y < top)
    to_up = y < top
    to_down = (y == 0, y <= 1)
    pass_far = (jnp.logical_and(y >= 1, y < top), jnp.logical_or(y == 0, y == top))
    from_side = jnp.logical_or(z == 1, y < top)
    from_down = y >= 1
    from_up = (y == top, jnp.logical_or(y == top, y == 0))
    from_far = y >= 2

    def both_parts(needed, step):
        step(0)

        @pl.when(needed)
        def _():
            step(1)

    def send(h, half, owner, peer, slot, needed):
        both_parts(needed, lambda part: kv_copy(h, half, part, owner, peer, slot).start())

    def sent(h, half, peer, slot, needed):
        both_parts(needed, lambda part: kv_copy(h, half, part, me, peer, slot).wait_send())

    def arrived(h, half, owner, needed):
        both_parts(needed, lambda part: kv_copy(h, half, part, owner, owner, 0).wait_recv())

    def send_own(h):
        for half in range(2):
            send(h, half, me, side, 0, to_side)
            send(h, half, me, up, 1, to_up)
            send(h, half, me, down, 2, to_down[half])

    def relay_near(h):
        for half in range(2):
            arrived(h, half, side, from_side)
            send(h, half, side, up, 3, to_up)
            send(h, half, side, down, 4, to_down[half])
            if half == 0:
                arrived(h, 0, down, from_down)
                send(h, 0, down, up, 5, pass_far[0])
            else:
                arrived(h, 1, up, from_up[1])
                send(h, 1, up, down, 5, pass_far[1])

    def relay_far(h):
        arrived(h, 0, side_down, from_down)
        send(h, 0, side_down, up, 6, pass_far[0])
        arrived(h, 1, side_up, from_up[1])
        send(h, 1, side_up, down, 6, pass_far[1])

    def await_half(h, half):
        if half == 0:
            arrived(h, 0, up, from_up[0])
            arrived(h, 0, side_up, from_up[0])
        else:
            arrived(h, 1, down, from_down)
            arrived(h, 1, side_down, from_down)
        arrived(h, half, far, from_far)
        arrived(h, half, side_far, from_far)

    def direct(half, step):
        for part in range(2):

            def one(i, _):
                peer = lax.rem(me + i, n)
                pl.when(jnp.logical_or(part == 0, peer > me))(lambda: step(kv_copy(0, half, part, me, peer, i - 1)))
                return 0

            lax.fori_loop(1, n, one, 0)

    def await_direct(half):
        def one(i, _):
            owner = lax.rem(me + i, n)
            arrived(0, half, owner, owner < me)
            return 0

        lax.fori_loop(1, n, one, 0)

    def r_copy(h, source, peer):
        return pltpu.make_async_remote_copy(
            src_ref=rsend.at[h, peer], dst_ref=rrecv.at[h, source],
            send_sem=r_send.at[h, peer], recv_sem=r_recv.at[h, source],
            device_id={"seq": peer}, device_id_type=MESH,
        )

    def load_queries(h, _):
        for g in range(GROUP):
            cols = pl.ds(pl.multiple_of((h * GROUP + g) * HD, HD), HD)
            x = q_in[:, cols].astype(f32) + bias_ref[pl.ds(h * GROUP + g, 1), :]
            q_s[h, g * tokens : (g + 1) * tokens, :] = (x * cosine + turn(x) * sine).astype(bf16)
        return 0

    def await_cache(h, _):
        fetch_cache(h, 0).wait()
        fetch_cache(h, 1).wait()
        return 0

    lax.fori_loop(0, KV, await_cache, 0)
    direct(0, lambda copy: copy.start())

    def begin_do(i, _):
        fetch_do(i // GROUP, lax.rem(i, GROUP)).start()
        return 0

    lax.fori_loop(0, KV * GROUP, begin_do, 0)
    fetch_q.wait()
    lax.fori_loop(0, KV, load_queries, 0)
    direct(1, lambda copy: copy.start())
    send_own(1)

    row = lax.broadcasted_iota(jnp.int32, (tokens, keys), 0)
    col = lax.broadcasted_iota(jnp.int32, (tokens, keys), 1)
    mask_ref[0] = jnp.where(col < start_ref[0], 0.0, -1e30)
    mask_ref[1] = jnp.where(col <= row + me * tokens, 0.0, -1e30)

    def more_tables(i, _):
        table(lax.rem(me + i, n))
        return 0

    lax.fori_loop(1, n, more_tables, 0)

    def finish(h):
        cols = pl.ds(pl.multiple_of(h * HD, HD), HD)

        def gather(source, total):
            r_copy(h, source, source).wait_recv()
            return total + rrecv[h, source].astype(f32)

        total = lax.fori_loop(me + 1, n, gather, rsend[h, me].astype(f32))
        gk_ref[:, cols] = (total[0] * cosine - turn(total[0]) * sine).astype(bf16)
        gv_ref[:, cols] = total[1].astype(bf16)

    early, late = slice(0, KV - 1), slice(KV - 1, KV)

    def exchange(size, index, device, buffer, send_sem, recv_sem):
        def copy(which, owner, peer):
            block = buffer.at[owner, (early, late)[which]]
            return pltpu.make_async_remote_copy(
                src_ref=block, dst_ref=block, send_sem=send_sem.at[which, peer], recv_sem=recv_sem.at[which, owner],
                device_id=device(peer), device_id_type=MESH,
            )

        def begin(which):
            def one(i, _):
                copy(which, index, lax.rem(index + i, size)).start()
                return 0

            lax.fori_loop(1, size, one, 0)

        def arrive(which):
            def one(i, _):
                peer = lax.rem(index + i, size)
                copy(which, peer, peer).wait_recv()
                return 0

            lax.fori_loop(1, size, one, 0)
            return jnp.sum(buffer[:, (early, late)[which]], axis=0)

        def leave(which):
            def one(i, _):
                copy(which, index, lax.rem(index + i, size)).wait_send()
                return 0

            lax.fori_loop(1, size, one, 0)

        return begin, arrive, leave

    begin_a, arrive_a, leave_a = exchange(n, me, lambda p: {"seq": p}, sum_a, a_send, a_recv)
    begin_b, arrive_b, leave_b = exchange(inner, lane, lambda p: {"dp": block * inner + p}, sum_b, b_send, b_recv)
    begin_c, arrive_c, leave_c = exchange(outer, block, lambda p: {"dp": p * inner + lane}, sum_c, c_send, c_recv)

    def head(h, _):
        last = h == KV - 1

        @pl.when(last)
        def _():
            begin_a(0)

        @pl.when(h == 0)
        def _():
            await_direct(0)

        @pl.when(h > 0)
        def _():
            await_half(h, 0)

        q_t[...] = q_s[h].T
        stat[...] = jnp.full(stat.shape, -3e38, f32)

        def score(part, _):
            s = dot(q_s[h], kv[h, 0, part].reshape(keys, HD), 1, 1)
            s = (s.reshape(GROUP, tokens, keys) + mask_ref[part][None]).reshape(rows, keys)
            s_ref[part] = s
            m = stat[...]
            for t in range(keys // HD):
                m = jnp.maximum(m, s[:, t * HD : (t + 1) * HD])
            stat[...] = m
            return 0

        for part in range(2):
            score(part, 0)

        @pl.when(h + 1 < KV)
        def _():
            relay_near(h + 1)


        stat[...] = jnp.broadcast_to(jnp.max(stat[...], axis=1, keepdims=True), stat.shape)

        @pl.when(h == 0)
        def _():
            await_direct(1)

        @pl.when(h > 0)
        def _():
            await_half(h, 1)


        def weigh(i, _):
            at = pl.ds(pl.multiple_of(i * (rows // 2), rows // 2), rows // 2)
            m = stat[at, :]
            total, product = 0.0, 0.0
            for part in range(2):
                pieces = [
                    jnp.exp2((s_ref[part, at, t * HD : (t + 1) * HD] - m) * EXP2_SCALE)
                    for t in range(keys // HD)
                ]
                total += functools.reduce(lambda a, b: a + b, pieces)
                p = jnp.concatenate([x.astype(bf16) for x in pieces], axis=1)
                p_ref[part, at, :] = p
                product += dot(p, kv[h, 1, part].reshape(keys, HD), 1, 0)
            norm[at, :] = total
            acc[at, :] = product
            return 0

        lax.fori_loop(0, 2, weigh, 0)

        @pl.when(h + 1 < KV)
        def _():
            relay_far(h + 1)

        @pl.when(h + 2 < KV)
        def _():
            send_own(h + 2)

        @pl.when(last)
        def _():
            sum_b[lane, early] = arrive_a(0)
            begin_b(0)

        def await_do(g, _):
            fetch_do(h, g).wait()
            return 0

        lax.fori_loop(0, GROUP, await_do, 0)
        inverse = 1.0 / jnp.sum(norm[...], axis=1, keepdims=True)
        out = (acc[...] * inverse).astype(bf16)
        for g in range(GROUP):
            cols = pl.ds(pl.multiple_of((h * GROUP + g) * HD, HD), HD)
            out_ref[:, cols] = out[g * tokens : (g + 1) * tokens]
        scaled = (do_s[h].astype(f32) * inverse).astype(bf16)
        do_n[...] = scaled
        do_t[...] = scaled.T
        delta = jnp.sum(scaled.astype(f32) * out.astype(f32), axis=1, keepdims=True)
        stat[...] = jnp.broadcast_to(delta, stat.shape)
        acc[...] = jnp.zeros(acc.shape, f32)

        def score_grad(part):
            dp = dot(do_n[...], kv[h, 1, part].reshape(keys, HD), 1, 1)
            delta = stat[...]
            ds = jnp.concatenate(
                [
                    (
                        (dp[:, t * HD : (t + 1) * HD] - delta)
                        * p_ref[part, :, t * HD : (t + 1) * HD].astype(f32)
                    ).astype(bf16)
                    for t in range(keys // HD)
                ],
                axis=1,
            )
            acc[...] += dot(ds, kv[h, 0, part].reshape(keys, HD), 1, 0)
            return ds

        ds = score_grad(1)
        dk = dot(q_t[...], ds, 1, 0).T * SCALE
        dv = dot(do_t[...], p_ref[1], 1, 0).T
        for r in range(n):
            rsend[h, r, 0] = dk[r * tokens : (r + 1) * tokens].astype(bf16)
            rsend[h, r, 1] = dv[r * tokens : (r + 1) * tokens].astype(bf16)

        def send_back(peer, _):
            r_copy(h, me, peer).start()
            return 0

        lax.fori_loop(0, me, send_back, 0)
        gk = dk * cos_s[...] - turn(dk) * sin_s[...]
        key_sums = [jnp.sum(gk, axis=0, keepdims=True), jnp.sum(dv, axis=0, keepdims=True)]
        score_grad(0)
        dq = (acc[...] * SCALE).astype(bf16).astype(f32)
        sums = []
        for g in range(GROUP):
            cols = pl.ds(pl.multiple_of((h * GROUP + g) * HD, HD), HD)
            x = dq[g * tokens : (g + 1) * tokens]
            gq = x * cosine - turn(x) * sine
            gq_ref[:, cols] = gq.astype(bf16)
            sums.append(jnp.sum(gq, axis=0, keepdims=True))
        filler = jnp.zeros((SLOTS - GROUP - 2, HD), f32)
        sum_a[me, h] = jnp.concatenate(sums + key_sums + [filler], axis=0)

        @pl.when(jnp.logical_and(h > 0, h + 1 < KV))
        def _():
            finish(h - 1)

        return 0

    lax.fori_loop(0, KV, head, 0)

    begin_a(1)
    finish(KV - 2)
    sum_c[block, early] = arrive_b(0)
    begin_c(0)
    sum_b[lane, late] = arrive_a(1)
    begin_b(1)
    finish(KV - 1)
    sum_c[block, late] = arrive_b(1)
    begin_c(1)

    def drain_head(h, _):
        for half in range(2):
            for slot, (peer, needed) in enumerate(
                (
                    (side, to_side), (up, to_up), (down, to_down[half]), (up, to_up), (down, to_down[half]),
                    (up if half == 0 else down, pass_far[half]), (up if half == 0 else down, pass_far[half]),
                )
            ):
                sent(h, half, peer, slot, needed)

        return 0

    def drain_back(h, _):
        def one(peer, _):
            r_copy(h, me, peer).wait_send()
            return 0

        return lax.fori_loop(0, me, one, 0)

    direct(0, lambda copy: copy.wait_send())
    direct(1, lambda copy: copy.wait_send())
    lax.fori_loop(1, KV, drain_head, 0)
    lax.fori_loop(0, KV, drain_back, 0)
    for which in range(2):
        leave_a(which)
        leave_b(which)
    sums_ref[early] = arrive_c(0)
    sums_ref[late] = arrive_c(1)
    leave_c(0)
    leave_c(1)


def store_kernel(*refs):
    count = len(refs) // 2
    sources, targets, sem = refs[:count], refs[count : 2 * count], refs[-1]
    copies = [pltpu.make_async_copy(a, b, sem.at[i]) for i, (a, b) in enumerate(zip(sources, targets))]
    for copy in copies:
        copy.start()
    for copy in copies:
        copy.wait()


def body(n, m, q_proj, k_proj, v_proj, cache_k, cache_v, bias_q, bias_k, bias_v, start, dout):
    tokens = q_proj.shape[1]
    keys, rows = n * tokens, GROUP * tokens
    inner = 8
    outer = m // inner
    bias = jnp.concatenate([bias_q, bias_k, bias_v]).astype(f32).reshape(SUMS, HD)
    vmem = pl.BlockSpec(memory_space=pltpu.VMEM)
    dma = pltpu.SemaphoreType.DMA
    out, grad_q, grad_k, grad_v, total = pl.pallas_call(
        functools.partial(attend_kernel, n, inner, outer),
        out_shape=[
            jax.ShapeDtypeStruct((tokens, HQ * HD), bf16),
            jax.ShapeDtypeStruct((tokens, HQ * HD), bf16),
            jax.ShapeDtypeStruct((tokens, KV * HD), bf16),
            jax.ShapeDtypeStruct((tokens, KV * HD), bf16),
            jax.ShapeDtypeStruct((KV, SLOTS, HD), f32),
        ],
        in_specs=[pl.BlockSpec(memory_space=pltpu.SMEM), vmem] + [pl.BlockSpec(memory_space=pltpu.HBM)] * 6,
        out_specs=[vmem] * 5,
        scratch_shapes=[
            pltpu.VMEM((tokens, HQ * HD), bf16),
            pltpu.VMEM((tokens, KV * HD), bf16),
            pltpu.VMEM((tokens, KV * HD), bf16),
            pltpu.VMEM((KV, 2, 2, n, tokens, HD), bf16),
            pltpu.VMEM((KV, n, 2, tokens, HD), bf16),
            pltpu.VMEM((KV, n, 2, tokens, HD), bf16),
            pltpu.VMEM((KV, rows, HD), bf16),
            pltpu.VMEM((KV, rows, HD), bf16),
            pltpu.VMEM((2, rows, keys), f32),
            pltpu.VMEM((2, rows, keys), bf16),
            pltpu.VMEM((2, tokens, keys), f32),
            pltpu.VMEM((rows, HD), f32),
            pltpu.VMEM((rows, HD), f32),
            pltpu.VMEM((rows, HD), f32),
            pltpu.VMEM((HD, rows), bf16),
            pltpu.VMEM((HD, rows), bf16),
            pltpu.VMEM((rows, HD), bf16),
            pltpu.VMEM((keys, HD), f32),
            pltpu.VMEM((keys, HD), f32),
            pltpu.VMEM((n, KV, SLOTS, HD), f32),
            pltpu.VMEM((inner, KV, SLOTS, HD), f32),
            pltpu.VMEM((outer, KV, SLOTS, HD), f32),
            dma((3,)),
            dma((KV, 2)),
            dma((KV, GROUP)),
            dma((KV, 2, 2, 7)),
            dma((KV, 2, 2, n)),
            dma((KV, n)),
            dma((KV, n)),
            dma((2, n)),
            dma((2, n)),
            dma((2, inner)),
            dma((2, inner)),
            dma((2, outer)),
            dma((2, outer)),
        ],
        compiler_params=pltpu.CompilerParams(collective_id=0, has_side_effects=True, vmem_limit_bytes=VMEM_LIMIT),
        name="attend",
    )(start, bias, *(pltpu.with_memory_space_constraint(x[0], pltpu.HBM) for x in (q_proj, k_proj, v_proj, cache_k, cache_v, dout)))
    anywhere, hbm = pl.BlockSpec(memory_space=pl.ANY), pl.BlockSpec(memory_space=pltpu.HBM)
    results = pl.pallas_call(
        store_kernel,
        out_shape=[jax.ShapeDtypeStruct(x.shape, x.dtype) for x in (out, grad_q, grad_k, grad_v)],
        in_specs=[anywhere] * 4,
        out_specs=[hbm] * 4,
        scratch_shapes=[dma((4,))],
        compiler_params=pltpu.CompilerParams(vmem_limit_bytes=1 << 20),
        name="store",
    )(out, grad_q, grad_k, grad_v)
    return (
        *(x[None] for x in results),
        total[:, :GROUP].reshape(HQ * HD), total[:, GROUP].reshape(KV * HD), total[:, GROUP + 1].reshape(KV * HD),
    )


VMEM_LIMIT = 44 << 20


def solution(mesh):
    n, m = mesh.shape["seq"], mesh.shape["dp"]
    tokens = P("dp", "seq", None)
    return jax.shard_map(
        functools.partial(body, n, m),
        mesh=mesh,
        in_specs=(tokens, tokens, tokens, tokens, tokens, P(), P(), P(), P("dp"), tokens),
        out_specs=(tokens, tokens, tokens, tokens, P(), P(), P()),
        check_vma=False,
    )
```
